32 devices in a mesh: vocab: 4 (over z), rows: 8 (over y, x, core).
Axes of the slice: x: 2, y: 2, z: 4, core: 2. Of those that a mesh axis runs over, the one named last changes fastest.
Arguments:
- trunk_hidden: bfloat16 [32, 7168], P('rows'), may hold values from -8 to 8
- mtp_state: bfloat16 [32, 7168], P('rows'), may hold values from -24 to 24, as said below
- mtp_gain: bfloat16 [7168], replicated, may hold values from 0.099609375 to 1.8984375
- head_weight: bfloat16 [4608, 7168], P(('vocab', 'rows')), may hold values from -0.28347335 to 0.28347335, as said below
- target_ids: int32 [32], replicated, may hold values from 0 to 4607
- mtp_target_ids: int32 [32], replicated, may hold values from 0 to 4607
- attn_values: bfloat16 [32, 16, 128], P('rows'), may hold values from -6 to 6
- out_proj: bfloat16 [2048, 7168], P('rows', 'vocab'), may hold values from -0.125 to 0.125
Outputs:
- grad_trunk: bfloat16 [32, 7168], P('rows')
- grad_residual: bfloat16 [32, 7168], P('rows')
- grad_gain: float32 [7168], replicated
- grad_head: bfloat16 [4608, 7168], P(('vocab', 'rows'))
- grad_attn: bfloat16 [32, 16, 128], P('vocab', 'rows')
- grad_out_proj: bfloat16 [2048, 7168], P('rows', 'vocab')
The draws below stay inside these ranges and needn't reach their ends.
Inputs may be any that keep to these rules, and one draw needn't show every extreme that they name: `mtp_state`: block outputs; rows differ in scale. `head_weight`: head rows.
All inputs are finite; a program needn't handle non-finite values.
Results may differ from the reference program's by a relative error of at most 0.025.
Values may be sent and summed in bfloat16 or wider, within the bound.
No kernel may reach another device: no remote copies, remote signals or barrier semaphores. Data moves between devices by JAX's collectives and lax.ppermute only.
A program may use at most 64 MiB of HBM per device.

```python
import math
import jax
import jax.numpy as jnp
import numpy as np
from jax import lax

D = 7168
VBLK = 144
HEAD_DIM = 128
TOKENS = 32
VOCAB = 4608
HEADS = 16


def head_table(key):
    raw = jax.random.normal(jax.random.fold_in(key, 101), (VOCAB, D), jnp.float32)
    return jnp.clip(raw, -6.0, 6.0) * (4.0 / math.sqrt(D))


def draw_head_weight(key, part):
    table = head_table(key)
    return table.astype(jnp.bfloat16)


def draw_trunk_hidden(key, part):
    base = jnp.clip(jax.random.normal(jax.random.fold_in(key, 102), (TOKENS, D), jnp.float32), -6.0, 6.0)
    return base.astype(jnp.bfloat16)


def draw_mtp_state(key, part):
    base = jnp.clip(jax.random.normal(jax.random.fold_in(key, 104), (TOKENS, D), jnp.float32), -6.0, 6.0)
    scales = jnp.exp(jax.random.uniform(jax.random.fold_in(key, 105), (TOKENS, 1), jnp.float32, math.log(0.3), math.log(3.0)))
    rows_out = base * scales
    return rows_out.astype(jnp.bfloat16)


def plant(values, stream_key, smallest, high):
    longest = values.shape.index(max(values.shape))
    spots = []
    for shift in (0, 1):
        where = [jax.random.randint(jax.random.fold_in(stream_key, axis), (), 0, length) for axis, length in enumerate(values.shape)]
        where[longest] = (where[longest] + shift) % values.shape[longest]
        spots.append(tuple(where))
    return values.at[spots[0]].set(smallest).at[spots[1]].set(high)


def shard_levels(key, shape, cuts, smallest, high):
    level = 1.0
    for axis_at, blocks in cuts:
        draws = jax.random.uniform(jax.random.fold_in(jax.random.fold_in(key, 6), axis_at), (blocks,), jnp.float32, smallest / len(cuts), high / len(cuts))
        level = level * jnp.repeat(jnp.exp(draws), shape[axis_at] // blocks).reshape((-1,) + (1,) * (len(shape) - 1 - axis_at))
    return level


def cumulative_ranks(amount, lean):
    portions = [(1 << 20) // math.isqrt(standing ** lean) + 1 for standing in range(1, amount + 1)]
    spread = 1 + sum(portions) // (1 << 30)
    return np.cumsum(np.array([max(1, weight // spread) for weight in portions]))


def ranked_ids(rng, dims, amount, lean):
    grid = cumulative_ranks(amount, lean)
    pick = jax.random.randint(jax.random.fold_in(rng, 1), dims, 0, int(grid[amount - 1]))
    rank = jnp.searchsorted(jnp.asarray(grid, jnp.int32), pick, side="right")
    return jax.random.permutation(jax.random.fold_in(rng, 2), amount)[rank].astype(jnp.int32)


def normal_values(rng, dims, deviation, reach, shards=(), held_as=jnp.bfloat16):
    values = jax.random.normal(rng, dims, jnp.float32) * deviation
    if len(shards) > 0:
        values = shard_levels(rng, dims, shards, -0.22, 0.18) * values
    return jnp.clip(values, min=-reach, max=reach).astype(held_as)


def setup_inputs(seed: int = 0) -> dict:
    key_of = jax.random.split(jax.random.key(seed), 9)
    trunk_hidden = draw_trunk_hidden(jax.random.fold_in(key_of[8], 71), 0)
    mtp_state = draw_mtp_state(jax.random.fold_in(key_of[8], 71), 0)
    mtp_gain = jnp.clip(1.0 + 0.18 * jax.random.normal(key_of[2], (D,), jnp.float32), 0.099609375, 1.8984375).astype(jnp.bfloat16)
    head_weight = draw_head_weight(jax.random.fold_in(key_of[8], 71), 0)
    target_ids = plant(ranked_ids(key_of[4], (TOKENS,), VOCAB, 2), jax.random.fold_in(key_of[4], 3), 0, VOCAB - 1).astype(jnp.int32)
    mtp_target_ids = plant(ranked_ids(key_of[5], (TOKENS,), VOCAB, 2), jax.random.fold_in(key_of[5], 3), 0, VOCAB - 1).astype(jnp.int32)
    attn_values = normal_values(key_of[6], (TOKENS, HEADS, HEAD_DIM), 1.0, 6.0, ((0, 8),))
    out_proj = normal_values(key_of[7], (HEADS * HEAD_DIM, D), (HEADS * HEAD_DIM) ** -0.5, 0.125, ((0, 8), (1, 4)))
    return dict(trunk_hidden=trunk_hidden, mtp_state=mtp_state, mtp_gain=mtp_gain, head_weight=head_weight, target_ids=target_ids, mtp_target_ids=mtp_target_ids, attn_values=attn_values, out_proj=out_proj)


loss_scale = 8.0
mtp_share = 0.3
norm_eps = 1e-06

def normalize(state):
    values = state.astype(jnp.float32)
    inverse = lax.rsqrt(lax.optimization_barrier(jnp.mean(values * values, axis=-1, keepdims=True)) + norm_eps)
    return (values * inverse, inverse)

def reference(trunk_hidden, mtp_state, mtp_gain, head_weight, target_ids, mtp_target_ids, attn_values, out_proj):
    gain = mtp_gain.astype(jnp.float32)
    normed, inverse = normalize(mtp_state)
    mtp_hidden = (normed * gain).astype(jnp.bfloat16)
    hidden = jnp.concatenate([trunk_hidden, mtp_hidden], axis=0)
    targets = jnp.concatenate([target_ids, mtp_target_ids]).astype(jnp.int32)
    shares = jnp.concatenate([jnp.full((TOKENS,), loss_scale, jnp.float32), jnp.full((TOKENS,), loss_scale * mtp_share, jnp.float32)])
    logits = lax.dot_general(hidden, head_weight, (((1,), (1,)), ((), ())), preferred_element_type=jnp.float32)
    top = lax.optimization_barrier(jnp.max(logits, axis=1, keepdims=True))
    total = lax.optimization_barrier(jnp.sum(jnp.exp(logits - top), axis=1, keepdims=True))
    onehot = (targets[:, None] == jnp.arange(VOCAB, dtype=jnp.int32)[None, :]).astype(jnp.float32)
    logit_grads = (shares[:, None] * (jnp.exp(logits - top) / total - onehot)).astype(jnp.bfloat16)
    blocks = VOCAB // VBLK
    weight_blocks = head_weight.reshape(blocks, VBLK, D)
    grad_blocks = logit_grads.reshape(2 * TOKENS, blocks, VBLK).transpose(1, 0, 2)

    def block_step(carry, pair):
        weight_block, grad_block = pair
        part = jnp.dot(grad_block, weight_block, preferred_element_type=jnp.float32).astype(jnp.bfloat16)
        part = lax.optimization_barrier(part).astype(jnp.float32)
        head_part = lax.dot_general(grad_block, hidden, (((0,), (0,)), ((), ())), preferred_element_type=jnp.float32).astype(jnp.bfloat16)
        return (carry + part, head_part)
    grad_hidden, head_parts = lax.scan(block_step, jnp.zeros((2 * TOKENS, D), jnp.float32), (weight_blocks, grad_blocks))
    grad_head = head_parts.reshape(VOCAB, D)
    grad_trunk = grad_hidden[:TOKENS].astype(jnp.bfloat16)
    mtp_grad = grad_hidden[TOKENS:]
    grad_gain = lax.optimization_barrier(jnp.sum(mtp_grad * normed, axis=0))
    scaled = mtp_grad * gain
    dot_mean = lax.optimization_barrier(jnp.mean(scaled * normed, axis=-1, keepdims=True))
    grad_residual = (inverse * (scaled - normed * dot_mean)).astype(jnp.bfloat16)
    grad_attn = lax.dot_general(grad_residual, out_proj, (((1,), (1,)), ((), ())), preferred_element_type=jnp.float32)
    grad_attn = grad_attn.astype(jnp.bfloat16).reshape(TOKENS, HEADS, HEAD_DIM)
    flat_values = attn_values.reshape(TOKENS, HEADS * HEAD_DIM)
    grad_out_proj = lax.dot_general(flat_values, grad_residual, (((0,), (0,)), ((), ())), preferred_element_type=jnp.float32).astype(jnp.bfloat16)
    return (grad_trunk, grad_residual, grad_gain, grad_head, grad_attn, grad_out_proj)
```

```python
import functools

import jax
import jax.numpy as jnp
from jax import lax
from jax.sharding import PartitionSpec as P

loss_scale = 8.0
mtp_share = 0.3
norm_eps = 1e-06


def swap(x, axis, k):
    n = lax.axis_size(axis)
    return lax.ppermute(x, axis, [(i, i ^ k) for i in range(n)])


def tree_sum(parts):
    while len(parts) > 1:
        parts = [a + b for a, b in zip(parts[::2], parts[1::2])]
    return parts[0]


def local(
    trunk_hidden,
    mtp_state,
    mtp_gain,
    head_weight,
    target_ids,
    mtp_target_ids,
    attn_values,
    out_proj,
):
    f32, bf16 = jnp.float32, jnp.bfloat16
    tok, width = trunk_hidden.shape
    nrow = lax.axis_size("rows")
    nvoc = lax.axis_size("vocab")
    ndev = nrow * nvoc
    nchip = nrow // 2
    row = lax.axis_index("rows")
    voc = lax.axis_index("vocab")
    core = row & 1
    chip = row >> 1
    vrows = head_weight.shape[0]
    cols = out_proj.shape[1]
    hdim = out_proj.shape[0]
    ntok = nrow * tok
    gain = mtp_gain.astype(f32)

    stacked = jnp.concatenate([trunk_hidden, mtp_state], axis=0)
    gathered = lax.all_gather(stacked, "rows", axis=0, tiled=True).reshape(nrow, 2, tok, width)
    state = gathered[:, 1].astype(f32)
    inverse = lax.rsqrt(jnp.mean(state * state, axis=-1, keepdims=True) + norm_eps)
    mtp_hidden = (state * inverse * gain).astype(bf16)
    hidden = jnp.stack([gathered[:, 0], mtp_hidden], axis=1).reshape(2 * ntok, width)

    targets = jnp.stack(
        [target_ids.reshape(nrow, tok), mtp_target_ids.reshape(nrow, tok)], axis=1
    ).reshape(-1)
    shares = jnp.broadcast_to(
        jnp.array([loss_scale, loss_scale * mtp_share], f32)[None, :, None], (nrow, 2, tok)
    ).reshape(-1)
    vocab_ids = (voc * nrow + row) * vrows + jnp.arange(vrows, dtype=jnp.int32)
    onehot = targets[:, None] == vocab_ids[None, :]

    logits = lax.dot_general(
        hidden, head_weight, (((1,), (1,)), ((), ())), preferred_element_type=f32
    )
    peak = jnp.max(logits, axis=1)
    below = logits - peak[:, None]
    weight = jnp.exp(below)
    mass = jnp.sum(weight, axis=1)
    moment = jnp.sum(weight * below, axis=1)
    picked = jnp.sum(jnp.where(onehot, logits, 0.0), axis=1)
    stats = jnp.stack([peak, mass, moment, picked])
    everyone = lax.all_to_all(
        jnp.broadcast_to(stats[None], (ndev,) + stats.shape),
        ("vocab", "rows"),
        split_axis=0,
        concat_axis=0,
        tiled=True,
    )
    peaks, masses, moments, picks = (everyone[:, k] for k in range(4))
    top = jnp.max(peaks, axis=0)
    drop = peaks - top
    factor = jnp.exp(drop)
    total = jnp.sum(factor * masses, axis=0)
    spread = jnp.sum(factor * (moments + drop * masses), axis=0) / total
    dot_mean = shares * (spread - (jnp.sum(picks, axis=0) - top)) / width
    dot_mean = dot_mean.reshape(nrow, 2, tok)[:, 1].reshape(ntok, 1)

    logit_grads = (
        shares[:, None] * (jnp.exp(logits - top[:, None]) / total[:, None] - onehot.astype(f32))
    ).astype(bf16)

    by_core = logit_grads.reshape(nchip, 2, 2, tok, vrows)

    def rows_for(which):
        part = lax.dynamic_index_in_dim(by_core, which, 1, keepdims=False)
        own = [lax.dynamic_index_in_dim(part, chip ^ j, 0, keepdims=False)[0] for j in range(nchip)]
        return jnp.concatenate([part[:, 1].reshape(nchip * tok, vrows)] + own, axis=0)

    def grads_of(rows):
        return jnp.dot(rows, head_weight, preferred_element_type=f32).astype(bf16)

    away = grads_of(rows_for(1 - core))
    kept = grads_of(rows_for(core))
    pair = (kept.astype(f32) + swap(away, "rows", 1).astype(f32)).astype(bf16)

    def columns_for(k):
        return lax.dynamic_slice_in_dim(pair, (voc ^ k) * cols, cols, 1)

    column_sum = tree_sum(
        [columns_for(0).astype(f32)]
        + [swap(columns_for(k), "vocab", k).astype(f32) for k in range(1, nvoc)]
    ).astype(bf16)
    nmod = nchip * tok
    module, main = column_sum[:nmod], column_sum[nmod:].reshape(nchip, tok, cols)
    plane = [jnp.concatenate([module, main[0]], axis=0)] + [
        swap(jnp.concatenate([module, main[j]], axis=0), "rows", 2 * j) for j in range(1, nchip)
    ]
    plane_sum = tree_sum([part.astype(f32) for part in plane]).astype(bf16)
    module, trunk_piece = plane_sum[:nmod], plane_sum[nmod:]
    other = swap(module, "rows", 1)

    grad_head = lax.dot_general(
        logit_grads, hidden, (((0,), (0,)), ((), ())), preferred_element_type=f32
    ).astype(bf16)
    values = lax.all_to_all(attn_values, "rows", split_axis=1, concat_axis=0, tiled=True)
    values = values.reshape(ntok, hdim)

    first = jnp.where(core == 0, module, other).reshape(nchip, 1, tok, cols)
    second = jnp.where(core == 0, other, module).reshape(nchip, 1, tok, cols)
    mtp_grad = jnp.concatenate([first, second], axis=1).reshape(ntok, cols).astype(f32)
    inv = inverse.reshape(ntok, 1)
    normed = lax.dynamic_slice_in_dim(
        gathered[:, 1].reshape(ntok, width), voc * cols, cols, 1
    ).astype(f32) * inv
    gain_piece = jnp.sum(mtp_grad * normed, axis=0, keepdims=True)
    scaled = mtp_grad * lax.dynamic_slice_in_dim(gain, voc * cols, cols, 0)
    residual = (inv * (scaled - normed * dot_mean)).astype(bf16)
    attn_terms = lax.dot_general(
        residual, out_proj, (((1,), (1,)), ((), ())), preferred_element_type=f32
    ).astype(bf16)
    grad_out_proj = lax.dot_general(
        values, residual, (((0,), (0,)), ((), ())), preferred_element_type=f32
    ).astype(bf16)

    residual_piece = lax.dynamic_slice_in_dim(residual, row * tok, tok, 0)
    gain_high = gain_piece.astype(bf16)
    gain_low = (gain_piece - gain_high.astype(f32)).astype(bf16)
    tok_voc = ntok // nvoc
    lines = -(-tok_voc * hdim // cols)
    terms = attn_terms.reshape(nvoc, tok_voc * hdim)
    terms = jnp.pad(terms, ((0, 0), (0, lines * cols - tok_voc * hdim))).reshape(nvoc, lines, cols)
    shared = jnp.concatenate([trunk_piece, residual_piece, gain_high, gain_low], axis=0)

    def parcel(k):
        mine = lax.dynamic_index_in_dim(terms, voc ^ k, 0, keepdims=False)
        return jnp.concatenate([shared, mine], axis=0)

    parcels = [parcel(0)] + [swap(parcel(k), "vocab", k) for k in range(1, nvoc)]
    ordered = jnp.stack(parcels)
    grad_attn = jnp.sum(ordered[:, 2 * tok + 2 :].astype(f32), axis=0).astype(bf16)
    grad_attn = grad_attn.reshape(-1)[: tok_voc * hdim].reshape(
        tok_voc, hdim // attn_values.shape[2], attn_values.shape[2]
    )
    pieces = [
        lax.dynamic_index_in_dim(ordered, voc ^ k, 0, keepdims=False)[: 2 * tok + 2]
        for k in range(nvoc)
    ]
    whole = jnp.concatenate(pieces, axis=1)
    grad_trunk = whole[:tok]
    grad_residual = whole[tok : 2 * tok]
    grad_gain = whole[2 * tok].astype(f32) + whole[2 * tok + 1].astype(f32)
    return (grad_trunk, grad_residual, grad_gain, grad_head, grad_attn, grad_out_proj)


def solution(mesh):
    return jax.shard_map(
        local,
        mesh=mesh,
        in_specs=(
            P("rows", None),
            P("rows", None),
            P(),
            P(("vocab", "rows"), None),
            P(),
            P(),
            P("rows", None, None),
            P("rows", "vocab"),
        ),
        out_specs=(
            P("rows", None),
            P("rows", None),
            P(),
            P(("vocab", "rows"), None),
            P("vocab", "rows", None),
            P("rows", "vocab"),
        ),
        check_vma=False,
    )
```

```python
import functools

import jax
import jax.numpy as jnp
from jax import lax
from jax.experimental import pallas as pl
from jax.experimental.pallas import tpu as pltpu
from jax.sharding import PartitionSpec as P

loss_scale = 8.0
mtp_share = 0.3
norm_eps = 1e-06


def swap(x, axis, k):
    n = lax.axis_size(axis)
    return lax.ppermute(x, axis, [(i, i ^ k) for i in range(n)])


def tree_sum(parts):
    while len(parts) > 1:
        parts = [a + b for a, b in zip(parts[::2], parts[1::2])]
    return parts[0]


def plain(
    trunk_hidden,
    mtp_state,
    mtp_gain,
    head_weight,
    target_ids,
    mtp_target_ids,
    attn_values,
    out_proj,
):
    f32, bf16 = jnp.float32, jnp.bfloat16
    tok, width = trunk_hidden.shape
    nrow = lax.axis_size("rows")
    nvoc = lax.axis_size("vocab")
    ndev = nrow * nvoc
    nchip = nrow // 2
    row = lax.axis_index("rows")
    voc = lax.axis_index("vocab")
    core = row & 1
    chip = row >> 1
    vrows = head_weight.shape[0]
    cols = out_proj.shape[1]
    hdim = out_proj.shape[0]
    ntok = nrow * tok
    gain = mtp_gain.astype(f32)

    stacked = jnp.concatenate([trunk_hidden, mtp_state], axis=0)
    gathered = lax.all_gather(stacked, "rows", axis=0, tiled=True).reshape(nrow, 2, tok, width)
    state = gathered[:, 1].astype(f32)
    inverse = lax.rsqrt(jnp.mean(state * state, axis=-1, keepdims=True) + norm_eps)
    mtp_hidden = (state * inverse * gain).astype(bf16)
    hidden = jnp.stack([gathered[:, 0], mtp_hidden], axis=1).reshape(2 * ntok, width)

    targets = jnp.stack(
        [target_ids.reshape(nrow, tok), mtp_target_ids.reshape(nrow, tok)], axis=1
    ).reshape(-1)
    shares = jnp.broadcast_to(
        jnp.array([loss_scale, loss_scale * mtp_share], f32)[None, :, None], (nrow, 2, tok)
    ).reshape(-1)
    vocab_ids = (voc * nrow + row) * vrows + jnp.arange(vrows, dtype=jnp.int32)
    onehot = targets[:, None] == vocab_ids[None, :]

    logits = lax.dot_general(
        hidden, head_weight, (((1,), (1,)), ((), ())), preferred_element_type=f32
    )
    peak = jnp.max(logits, axis=1)
    below = logits - peak[:, None]
    weight = jnp.exp(below)
    mass = jnp.sum(weight, axis=1)
    moment = jnp.sum(weight * below, axis=1)
    picked = jnp.sum(jnp.where(onehot, logits, 0.0), axis=1)
    stats = jnp.stack([peak, mass, moment, picked])
    everyone = lax.all_to_all(
        jnp.broadcast_to(stats[None], (ndev,) + stats.shape),
        ("vocab", "rows"),
        split_axis=0,
        concat_axis=0,
        tiled=True,
    )
    peaks, masses, moments, picks = (everyone[:, k] for k in range(4))
    top = jnp.max(peaks, axis=0)
    drop = peaks - top
    factor = jnp.exp(drop)
    total = jnp.sum(factor * masses, axis=0)
    spread = jnp.sum(factor * (moments + drop * masses), axis=0) / total
    dot_mean = shares * (spread - (jnp.sum(picks, axis=0) - top)) / width
    dot_mean = dot_mean.reshape(nrow, 2, tok)[:, 1].reshape(ntok, 1)

    logit_grads = (
        shares[:, None] * (jnp.exp(logits - top[:, None]) / total[:, None] - onehot.astype(f32))
    ).astype(bf16)

    by_core = logit_grads.reshape(nchip, 2, 2, tok, vrows)

    def rows_for(which):
        part = lax.dynamic_index_in_dim(by_core, which, 1, keepdims=False)
        own = [lax.dynamic_index_in_dim(part, chip ^ j, 0, keepdims=False)[0] for j in range(nchip)]
        return jnp.concatenate([part[:, 1].reshape(nchip * tok, vrows)] + own, axis=0)

    def grads_of(rows):
        return jnp.dot(rows, head_weight, preferred_element_type=f32).astype(bf16)

    away = grads_of(rows_for(1 - core))
    kept = grads_of(rows_for(core))
    pair = (kept.astype(f32) + swap(away, "rows", 1).astype(f32)).astype(bf16)

    def columns_for(k):
        return lax.dynamic_slice_in_dim(pair, (voc ^ k) * cols, cols, 1)

    column_sum = tree_sum(
        [columns_for(0).astype(f32)]
        + [swap(columns_for(k), "vocab", k).astype(f32) for k in range(1, nvoc)]
    ).astype(bf16)
    nmod = nchip * tok
    module, main = column_sum[:nmod], column_sum[nmod:].reshape(nchip, tok, cols)
    plane = [jnp.concatenate([module, main[0]], axis=0)] + [
        swap(jnp.concatenate([module, main[j]], axis=0), "rows", 2 * j) for j in range(1, nchip)
    ]
    plane_sum = tree_sum([part.astype(f32) for part in plane]).astype(bf16)
    module, trunk_piece = plane_sum[:nmod], plane_sum[nmod:]
    other = swap(module, "rows", 1)

    grad_head = lax.dot_general(
        logit_grads, hidden, (((0,), (0,)), ((), ())), preferred_element_type=f32
    ).astype(bf16)
    values = lax.all_to_all(attn_values, "rows", split_axis=1, concat_axis=0, tiled=True)
    values = values.reshape(ntok, hdim)

    first = jnp.where(core == 0, module, other).reshape(nchip, 1, tok, cols)
    second = jnp.where(core == 0, other, module).reshape(nchip, 1, tok, cols)
    mtp_grad = jnp.concatenate([first, second], axis=1).reshape(ntok, cols).astype(f32)
    inv = inverse.reshape(ntok, 1)
    normed = lax.dynamic_slice_in_dim(
        gathered[:, 1].reshape(ntok, width), voc * cols, cols, 1
    ).astype(f32) * inv
    gain_piece = jnp.sum(mtp_grad * normed, axis=0, keepdims=True)
    scaled = mtp_grad * lax.dynamic_slice_in_dim(gain, voc * cols, cols, 0)
    residual = (inv * (scaled - normed * dot_mean)).astype(bf16)
    attn_terms = lax.dot_general(
        residual, out_proj, (((1,), (1,)), ((), ())), preferred_element_type=f32
    ).astype(bf16)
    grad_out_proj = lax.dot_general(
        values, residual, (((0,), (0,)), ((), ())), preferred_element_type=f32
    ).astype(bf16)

    residual_piece = lax.dynamic_slice_in_dim(residual, row * tok, tok, 0)
    gain_high = gain_piece.astype(bf16)
    gain_low = (gain_piece - gain_high.astype(f32)).astype(bf16)
    tok_voc = ntok // nvoc
    lines = -(-tok_voc * hdim // cols)
    terms = attn_terms.reshape(nvoc, tok_voc * hdim)
    terms = jnp.pad(terms, ((0, 0), (0, lines * cols - tok_voc * hdim))).reshape(nvoc, lines, cols)
    shared = jnp.concatenate([trunk_piece, residual_piece, gain_high, gain_low], axis=0)

    def parcel(k):
        mine = lax.dynamic_index_in_dim(terms, voc ^ k, 0, keepdims=False)
        return jnp.concatenate([shared, mine], axis=0)

    parcels = [parcel(0)] + [swap(parcel(k), "vocab", k) for k in range(1, nvoc)]
    ordered = jnp.stack(parcels)
    grad_attn = jnp.sum(ordered[:, 2 * tok + 2 :].astype(f32), axis=0).astype(bf16)
    grad_attn = grad_attn.reshape(-1)[: tok_voc * hdim].reshape(
        tok_voc, hdim // attn_values.shape[2], attn_values.shape[2]
    )
    pieces = [
        lax.dynamic_index_in_dim(ordered, voc ^ k, 0, keepdims=False)[: 2 * tok + 2]
        for k in range(nvoc)
    ]
    whole = jnp.concatenate(pieces, axis=1)
    grad_trunk = whole[:tok]
    grad_residual = whole[tok : 2 * tok]
    grad_gain = whole[2 * tok].astype(f32) + whole[2 * tok + 1].astype(f32)
    return (grad_trunk, grad_residual, grad_gain, grad_head, grad_attn, grad_out_proj)


NT = (((1,), (1,)), ((), ()))
NN = (((1,), (0,)), ((), ()))


def iota(shape, dim):
    return lax.broadcasted_iota(jnp.int32, shape, dim)


def matmul(a, b, dims=NN):
    return lax.dot_general(a, b, dims, preferred_element_type=jnp.float32)


def onehot(mask):
    return jnp.where(mask, 1.0, 0.0).astype(jnp.bfloat16)


def chunks(width):
    step = next(s for s in (1024, 512, 256, 128) if width % s == 0)
    return [slice(c, c + step) for c in range(0, width, step)]


def kernel_call(body, outs, *args, side=None):
    vmem = pl.BlockSpec(memory_space=pltpu.VMEM)
    return pl.pallas_call(
        body,
        in_specs=[vmem] * len(args),
        out_specs=[vmem] * len(outs),
        out_shape=[jax.ShapeDtypeStruct(s, d) for s, d in outs],
        scratch_shapes=side or [],
        compiler_params=pltpu.CompilerParams(vmem_limit_bytes=16 << 20),
    )(*args)


def head_kernel(tok, x_ref, w_ref, gain_ref, ids_ref, mids_ref, hid_ref, lt_ref, tgt_ref, inv_ref, msg_ref):
    f32, bf16 = jnp.float32, jnp.bfloat16
    rows, width = x_ref.shape
    vrows = w_ref.shape[0]
    half = rows // 2
    module = (iota((rows, 1), 0) // tok) % 2 == 1
    square = jnp.zeros((rows, 1), f32)
    for c in chunks(width):
        x = x_ref[:, c].astype(f32)
        square += jnp.sum(x * x, axis=1, keepdims=True)
    inverse = lax.rsqrt(square / width + norm_eps)
    inv_ref[...] = inverse
    lt = jnp.zeros((vrows, rows), f32)
    for c in chunks(width):
        x = x_ref[:, c].astype(f32)
        h = jnp.where(module, x * inverse * gain_ref[:, c].astype(f32), x).astype(bf16)
        hid_ref[:, c] = h
        lt += matmul(w_ref[:, c], h, NT)
    lt_ref[...] = lt
    eye = iota((half, half), 0) == iota((half, half), 1)
    main = jnp.sum(jnp.where(eye, ids_ref[...], 0), axis=1, keepdims=True)
    other = jnp.sum(jnp.where(eye, mids_ref[...], 0), axis=1, keepdims=True)
    src, dst = iota((half, rows), 0), iota((half, rows), 1)
    place = (src // tok) * 2 * tok + src % tok
    tgt = jnp.where(dst == place, main, 0) + jnp.where(dst == place + tok, other, 0)
    tgt = jnp.sum(tgt, axis=0, keepdims=True)
    base = (lax.axis_index("vocab") * lax.axis_size("rows") + lax.axis_index("rows")) * vrows
    tgt = tgt - base
    tgt_ref[...] = tgt
    peak = jnp.max(lt, axis=0, keepdims=True)
    below = lt - peak
    weight = jnp.exp(below)
    picked = jnp.where(iota((vrows, rows), 0) == tgt, lt, 0.0)
    slot = msg_ref.shape[1] // 4
    msg_ref[...] = jnp.zeros(msg_ref.shape, f32)
    for k, stat in enumerate(
        (
            peak,
            jnp.sum(weight, axis=0, keepdims=True),
            jnp.sum(weight * below, axis=0, keepdims=True),
            jnp.sum(picked, axis=0, keepdims=True),
        )
    ):
        msg_ref[:, k * slot : k * slot + rows] = jnp.broadcast_to(stat, (msg_ref.shape[0], rows))


def loss_kernel(tok, cols, ev_ref, lt_ref, tgt_ref, w_ref, gt_ref, dot_ref, away_ref, keep_ref):
    f32, bf16 = jnp.float32, jnp.bfloat16
    vrows, rows = lt_ref.shape
    width = w_ref.shape[1]
    slot = ev_ref.shape[1] // 4
    row, voc = lax.axis_index("rows"), lax.axis_index("vocab")
    core, chip = row % 2, row // 2
    peaks, masses, moments, picks = (ev_ref[:, k * slot : k * slot + rows] for k in range(4))
    top = jnp.max(peaks, axis=0, keepdims=True)
    drop = peaks - top
    factor = jnp.exp(drop)
    total = jnp.sum(factor * masses, axis=0, keepdims=True)
    spread = jnp.sum(factor * (moments + drop * masses), axis=0, keepdims=True) / total
    module = (iota((1, rows), 1) // tok) % 2 == 1
    share = jnp.where(module, loss_scale * mtp_share, loss_scale).astype(f32)
    dot_mean = share * (spread - (jnp.sum(picks, axis=0, keepdims=True) - top)) / width
    dot_mean = jnp.where(module, dot_mean, 0.0)
    eye = iota((rows, rows), 0) == iota((rows, rows), 1)
    dot_ref[...] = jnp.sum(jnp.where(eye, dot_mean, 0.0), axis=1, keepdims=True)
    hit = jnp.where(iota((vrows, rows), 0) == tgt_ref[...], 1.0, 0.0)
    gt = (share * (jnp.exp(lt_ref[...] - top) / total - hit)).astype(bf16)
    gt_ref[...] = gt
    line, col = iota((rows, rows), 0), iota((rows, rows), 1)
    half, quarter = rows // 2, rows // 4
    who = jnp.where(line < half, core, 1 - core)
    spot = line % half
    mod_spot = spot < quarter
    block = (spot % quarter) // tok
    owner = jnp.where(mod_spot, block, block ^ chip)
    want = (2 * owner + who) * 2 * tok + jnp.where(mod_spot, tok, 0) + spot % tok
    grads = matmul(onehot(col == want), gt, NT).astype(bf16)
    for k in range(width // cols):
        start = pl.multiple_of((voc ^ k) * cols, 128)
        part = matmul(grads, w_ref[:, pl.ds(start, cols)])
        keep_ref[k] = part[:half].astype(bf16)
        away_ref[k] = part[half:].astype(bf16)


def pair_kernel(keep_ref, got_ref, *outs):
    for k, out in enumerate(outs):
        out[...] = (keep_ref[k].astype(jnp.float32) + got_ref[k].astype(jnp.float32)).astype(
            jnp.bfloat16
        )


def column_kernel(tok, nvoc, *refs):
    parts, outs = refs[:nvoc], refs[nvoc:]
    total = tree_sum([p[...].astype(jnp.float32) for p in parts])
    nmod = len(outs) * tok
    for j, out in enumerate(outs):
        main = total[nmod + j * tok : nmod + (j + 1) * tok]
        out[...] = jnp.concatenate([total[:nmod], main], axis=0).astype(jnp.bfloat16)


def plane_kernel(nchip, *refs):
    parts, (mod_ref, trunk_ref) = refs[:nchip], refs[nchip:]
    total = tree_sum([p[...].astype(jnp.float32) for p in parts])
    nmod = mod_ref.shape[0]
    mod_ref[...] = total[:nmod].astype(jnp.bfloat16)
    trunk_ref[...] = total[nmod:].astype(jnp.bfloat16)


def last_kernel(tok, x_ref, inv_ref, dot_ref, gain_ref, proj_ref, own_ref, other_ref, trunk_ref, res_ref, *outs):
    f32, bf16 = jnp.float32, jnp.bfloat16
    parcels, (scratch,) = outs[:-1], outs[-1:]
    rows = x_ref.shape[0]
    half = rows // 2
    hdim, cols = proj_ref.shape
    nmod = own_ref.shape[0]
    nvoc = len(parcels)
    row, voc = lax.axis_index("rows"), lax.axis_index("vocab")
    core = row % 2
    line, spot = iota((rows, nmod), 0), iota((rows, nmod), 1)
    owner = line // (2 * tok)
    same = (line // tok) % 2 == 1
    same &= spot == (owner // 2) * tok + line % tok
    grad = matmul(onehot(same & (owner % 2 == core)), own_ref[...])
    grad += matmul(onehot(same & (owner % 2 != core)), other_ref[...])
    start = pl.multiple_of(voc * cols, 128)
    inverse = inv_ref[...]
    normed = x_ref[:, pl.ds(start, cols)].astype(f32) * inverse
    gain_piece = jnp.sum(grad * normed, axis=0, keepdims=True)
    scaled = grad * gain_ref[:, pl.ds(start, cols)].astype(f32)
    wide = (inverse * (scaled - normed * dot_ref[...])).astype(bf16)
    line, spot = iota((half, rows), 0), iota((half, rows), 1)
    residual = matmul(onehot(spot == (line // tok) * 2 * tok + tok + line % tok), wide).astype(bf16)
    res_ref[...] = residual
    terms = matmul(residual, proj_ref[...], NT)
    lines = parcels[0].shape[0]
    line = iota((lines, 1), 0)
    mine = matmul(
        onehot(
            (iota((lines, half), 0) - tok + row * tok == iota((lines, half), 1))
            & (line >= tok)
            & (line < 2 * tok)
        ),
        residual,
    )
    mine += matmul(onehot(iota((lines, tok), 0) == iota((lines, tok), 1)), trunk_ref[...])
    high = gain_piece.astype(bf16).astype(f32)
    mine += jnp.where(line == 2 * tok, high, 0.0) + jnp.where(
        line == 2 * tok + 1, gain_piece - high, 0.0
    )
    scratch[...] = terms
    tok_voc = half // nvoc
    per = cols // hdim
    for k, out in enumerate(parcels):
        block = scratch[pl.ds(pl.multiple_of((voc ^ k) * tok_voc, tok_voc), tok_voc), :]
        total = mine
        for j in range(-(-tok_voc // per)):
            lane = [block[i : i + 1] for i in range(j * per, min((j + 1) * per, tok_voc))]
            if len(lane) * hdim < cols:
                lane.append(jnp.zeros((1, cols - len(lane) * hdim), f32))
            total = total + jnp.where(line == 2 * tok + 2 + j, jnp.concatenate(lane, axis=1), 0.0)
        out[...] = total.astype(bf16)


def output_kernel(tok, nvoc, *refs):
    f32, bf16 = jnp.float32, jnp.bfloat16
    parts, (trunk_ref, res_ref, gain_ref, attn_ref) = refs[:nvoc], refs[nvoc:]
    cols = parts[0].shape[1]
    voc = lax.axis_index("vocab")
    values = [p[...].astype(f32) for p in parts]
    for k, part in enumerate(values):
        at = pl.ds(pl.multiple_of((voc ^ k) * cols, 128), cols)
        trunk_ref[:, at] = part[:tok].astype(bf16)
        res_ref[:, at] = part[tok : 2 * tok].astype(bf16)
        gain_ref[:, at] = part[2 * tok : 2 * tok + 1] + part[2 * tok + 1 : 2 * tok + 2]
    total = tree_sum(values)
    count, heads, size = attn_ref.shape
    per = cols // (heads * size)
    for i in range(count):
        line = 2 * tok + 2 + i // per
        at = (i % per) * heads * size
        attn_ref[i] = jnp.concatenate(
            [total[line : line + 1, at + h * size : at + (h + 1) * size] for h in range(heads)],
            axis=0,
        ).astype(bf16)


def local(
    trunk_hidden,
    mtp_state,
    mtp_gain,
    head_weight,
    target_ids,
    mtp_target_ids,
    attn_values,
    out_proj,
):
    f32, bf16 = jnp.float32, jnp.bfloat16
    tok, width = trunk_hidden.shape
    nrow = lax.axis_size("rows")
    nvoc = lax.axis_size("vocab")
    nchip = nrow // 2
    vrows = head_weight.shape[0]
    hdim, cols = out_proj.shape
    ntok = nrow * tok
    part = functools.partial
    gain = mtp_gain.reshape(1, width)
    slot = -(-2 * ntok // 128) * 128

    stacked = jnp.concatenate([trunk_hidden, mtp_state], axis=0)
    gathered = lax.all_gather(stacked, "rows", axis=0, tiled=True)
    hidden, logits, targets, inverse, stats = kernel_call(
        part(head_kernel, tok),
        [
            ((2 * ntok, width), bf16),
            ((vrows, 2 * ntok), f32),
            ((1, 2 * ntok), jnp.int32),
            ((2 * ntok, 1), f32),
            ((nrow * nvoc, 4 * slot), f32),
        ],
        gathered,
        head_weight,
        gain,
        target_ids.reshape(1, ntok),
        mtp_target_ids.reshape(1, ntok),
    )
    everyone = lax.all_to_all(
        stats, ("vocab", "rows"), split_axis=0, concat_axis=0, tiled=True
    )
    logit_grads, dot_mean, away, keep = kernel_call(
        part(loss_kernel, tok, cols),
        [
            ((vrows, 2 * ntok), bf16),
            ((2 * ntok, 1), f32),
            ((nvoc, ntok, cols), bf16),
            ((nvoc, ntok, cols), bf16),
        ],
        everyone,
        logits,
        targets,
        head_weight,
    )
    got = swap(away, "rows", 1)
    grad_head = lax.dot_general(
        logit_grads, hidden, (((1,), (0,)), ((), ())), preferred_element_type=f32
    ).astype(bf16)
    pair = kernel_call(pair_kernel, [((ntok, cols), bf16)] * nvoc, keep, got)
    column = [pair[0]] + [swap(pair[k], "vocab", k) for k in range(1, nvoc)]
    nmod = nchip * tok
    plane = kernel_call(
        part(column_kernel, tok, nvoc), [((nmod + tok, cols), bf16)] * nchip, *column
    )
    plane = [plane[0]] + [swap(plane[j], "rows", 2 * j) for j in range(1, nchip)]
    module, trunk_piece = kernel_call(
        part(plane_kernel, nchip), [((nmod, cols), bf16), ((tok, cols), bf16)], *plane
    )
    other = swap(module, "rows", 1)
    values = lax.all_to_all(attn_values, "rows", split_axis=1, concat_axis=0, tiled=True)

    tok_voc = ntok // nvoc
    lines = 2 * tok + 2 + -(-tok_voc // (cols // hdim))
    lines = -(-lines // 8) * 8
    residual, *parcels = kernel_call(
        part(last_kernel, tok),
        [((ntok, cols), bf16)] + [((lines, cols), bf16)] * nvoc,
        gathered,
        inverse,
        dot_mean,
        gain,
        out_proj,
        module,
        other,
        trunk_piece,
        side=[pltpu.VMEM((ntok, hdim), f32)],
    )
    parcels = [parcels[0]] + [swap(parcels[k], "vocab", k) for k in range(1, nvoc)]
    grad_out_proj = lax.dot_general(
        values.reshape(ntok, hdim), residual, (((0,), (0,)), ((), ())), preferred_element_type=f32
    ).astype(bf16)
    size = attn_values.shape[2]
    grad_trunk, grad_residual, grad_gain, grad_attn = kernel_call(
        part(output_kernel, tok, nvoc),
        [
            ((tok, width), bf16),
            ((tok, width), bf16),
            ((1, width), f32),
            ((tok_voc, hdim // size, size), bf16),
        ],
        *parcels,
    )
    return (
        grad_trunk,
        grad_residual,
        grad_gain.reshape(width),
        grad_head,
        grad_attn,
        grad_out_proj,
    )


def choose(*args):
    tok, cols, hdim = args[0].shape[0], args[7].shape[1], args[7].shape[0]
    fits = cols % 128 == 0 and hdim <= cols and (lax.axis_size("rows") * tok) % lax.axis_size("vocab") == 0
    return local(*args) if fits else plain(*args)


def solution(mesh):
    return jax.shard_map(
        choose,
        mesh=mesh,
        in_specs=(
            P("rows", None),
            P("rows", None),
            P(),
            P(("vocab", "rows"), None),
            P(),
            P(),
            P("rows", None, None),
            P("rows", "vocab"),
        ),
        out_specs=(
            P("rows", None),
            P("rows", None),
            P(),
            P(("vocab", "rows"), None),
            P("vocab", "rows", None),
            P("rows", "vocab"),
        ),
        check_vma=False,
    )
```

```python
import functools

import jax
import jax.numpy as jnp
from jax import lax
from jax.experimental import pallas as pl
from jax.experimental.pallas import tpu as pltpu
from jax.sharding import PartitionSpec as P

loss_scale = 8.0
mtp_share = 0.3
norm_eps = 1e-06


def swap(x, axis, k):
    n = lax.axis_size(axis)
    return lax.ppermute(x, axis, [(i, i ^ k) for i in range(n)])


def tree_sum(parts):
    while len(parts) > 1:
        parts = [a + b for a, b in zip(parts[::2], parts[1::2])]
    return parts[0]


def plain(
    trunk_hidden,
    mtp_state,
    mtp_gain,
    head_weight,
    target_ids,
    mtp_target_ids,
    attn_values,
    out_proj,
):
    f32, bf16 = jnp.float32, jnp.bfloat16
    tok, width = trunk_hidden.shape
    nrow = lax.axis_size("rows")
    nvoc = lax.axis_size("vocab")
    ndev = nrow * nvoc
    nchip = nrow // 2
    row = lax.axis_index("rows")
    voc = lax.axis_index("vocab")
    core = row & 1
    chip = row >> 1
    vrows = head_weight.shape[0]
    cols = out_proj.shape[1]
    hdim = out_proj.shape[0]
    ntok = nrow * tok
    gain = mtp_gain.astype(f32)

    stacked = jnp.concatenate([trunk_hidden, mtp_state], axis=0)
    gathered = lax.all_gather(stacked, "rows", axis=0, tiled=True).reshape(nrow, 2, tok, width)
    state = gathered[:, 1].astype(f32)
    inverse = lax.rsqrt(jnp.mean(state * state, axis=-1, keepdims=True) + norm_eps)
    mtp_hidden = (state * inverse * gain).astype(bf16)
    hidden = jnp.stack([gathered[:, 0], mtp_hidden], axis=1).reshape(2 * ntok, width)

    targets = jnp.stack(
        [target_ids.reshape(nrow, tok), mtp_target_ids.reshape(nrow, tok)], axis=1
    ).reshape(-1)
    shares = jnp.broadcast_to(
        jnp.array([loss_scale, loss_scale * mtp_share], f32)[None, :, None], (nrow, 2, tok)
    ).reshape(-1)
    vocab_ids = (voc * nrow + row) * vrows + jnp.arange(vrows, dtype=jnp.int32)
    onehot = targets[:, None] == vocab_ids[None, :]

    logits = lax.dot_general(
        hidden, head_weight, (((1,), (1,)), ((), ())), preferred_element_type=f32
    )
    peak = jnp.max(logits, axis=1)
    below = logits - peak[:, None]
    weight = jnp.exp(below)
    mass = jnp.sum(weight, axis=1)
    moment = jnp.sum(weight * below, axis=1)
    picked = jnp.sum(jnp.where(onehot, logits, 0.0), axis=1)
    stats = jnp.stack([peak, mass, moment, picked])
    everyone = lax.all_to_all(
        jnp.broadcast_to(stats[None], (ndev,) + stats.shape),
        ("vocab", "rows"),
        split_axis=0,
        concat_axis=0,
        tiled=True,
    )
    peaks, masses, moments, picks = (everyone[:, k] for k in range(4))
    top = jnp.max(peaks, axis=0)
    drop = peaks - top
    factor = jnp.exp(drop)
    total = jnp.sum(factor * masses, axis=0)
    spread = jnp.sum(factor * (moments + drop * masses), axis=0) / total
    dot_mean = shares * (spread - (jnp.sum(picks, axis=0) - top)) / width
    dot_mean = dot_mean.reshape(nrow, 2, tok)[:, 1].reshape(ntok, 1)

    logit_grads = (
        shares[:, None] * (jnp.exp(logits - top[:, None]) / total[:, None] - onehot.astype(f32))
    ).astype(bf16)

    by_core = logit_grads.reshape(nchip, 2, 2, tok, vrows)

    def rows_for(which):
        part = lax.dynamic_index_in_dim(by_core, which, 1, keepdims=False)
        own = [lax.dynamic_index_in_dim(part, chip ^ j, 0, keepdims=False)[0] for j in range(nchip)]
        return jnp.concatenate([part[:, 1].reshape(nchip * tok, vrows)] + own, axis=0)

    def grads_of(rows):
        return jnp.dot(rows, head_weight, preferred_element_type=f32).astype(bf16)

    away = grads_of(rows_for(1 - core))
    kept = grads_of(rows_for(core))
    pair = (kept.astype(f32) + swap(away, "rows", 1).astype(f32)).astype(bf16)

    def columns_for(k):
        return lax.dynamic_slice_in_dim(pair, (voc ^ k) * cols, cols, 1)

    column_sum = tree_sum(
        [columns_for(0).astype(f32)]
        + [swap(columns_for(k), "vocab", k).astype(f32) for k in range(1, nvoc)]
    ).astype(bf16)
    nmod = nchip * tok
    module, main = column_sum[:nmod], column_sum[nmod:].reshape(nchip, tok, cols)
    plane = [jnp.concatenate([module, main[0]], axis=0)] + [
        swap(jnp.concatenate([module, main[j]], axis=0), "rows", 2 * j) for j in range(1, nchip)
    ]
    plane_sum = tree_sum([part.astype(f32) for part in plane]).astype(bf16)
    module, trunk_piece = plane_sum[:nmod], plane_sum[nmod:]
    other = swap(module, "rows", 1)

    grad_head = lax.dot_general(
        logit_grads, hidden, (((0,), (0,)), ((), ())), preferred_element_type=f32
    ).astype(bf16)
    values = lax.all_to_all(attn_values, "rows", split_axis=1, concat_axis=0, tiled=True)
    values = values.reshape(ntok, hdim)

    first = jnp.where(core == 0, module, other).reshape(nchip, 1, tok, cols)
    second = jnp.where(core == 0, other, module).reshape(nchip, 1, tok, cols)
    mtp_grad = jnp.concatenate([first, second], axis=1).reshape(ntok, cols).astype(f32)
    inv = inverse.reshape(ntok, 1)
    normed = lax.dynamic_slice_in_dim(
        gathered[:, 1].reshape(ntok, width), voc * cols, cols, 1
    ).astype(f32) * inv
    gain_piece = jnp.sum(mtp_grad * normed, axis=0, keepdims=True)
    scaled = mtp_grad * lax.dynamic_slice_in_dim(gain, voc * cols, cols, 0)
    residual = (inv * (scaled - normed * dot_mean)).astype(bf16)
    attn_terms = lax.dot_general(
        residual, out_proj, (((1,), (1,)), ((), ())), preferred_element_type=f32
    ).astype(bf16)
    grad_out_proj = lax.dot_general(
        values, residual, (((0,), (0,)), ((), ())), preferred_element_type=f32
    ).astype(bf16)

    residual_piece = lax.dynamic_slice_in_dim(residual, row * tok, tok, 0)
    gain_high = gain_piece.astype(bf16)
    gain_low = (gain_piece - gain_high.astype(f32)).astype(bf16)
    tok_voc = ntok // nvoc
    lines = -(-tok_voc * hdim // cols)
    terms = attn_terms.reshape(nvoc, tok_voc * hdim)
    terms = jnp.pad(terms, ((0, 0), (0, lines * cols - tok_voc * hdim))).reshape(nvoc, lines, cols)
    shared = jnp.concatenate([trunk_piece, residual_piece, gain_high, gain_low], axis=0)

    def parcel(k):
        mine = lax.dynamic_index_in_dim(terms, voc ^ k, 0, keepdims=False)
        return jnp.concatenate([shared, mine], axis=0)

    parcels = [parcel(0)] + [swap(parcel(k), "vocab", k) for k in range(1, nvoc)]
    ordered = jnp.stack(parcels)
    grad_attn = jnp.sum(ordered[:, 2 * tok + 2 :].astype(f32), axis=0).astype(bf16)
    grad_attn = grad_attn.reshape(-1)[: tok_voc * hdim].reshape(
        tok_voc, hdim // attn_values.shape[2], attn_values.shape[2]
    )
    pieces = [
        lax.dynamic_index_in_dim(ordered, voc ^ k, 0, keepdims=False)[: 2 * tok + 2]
        for k in range(nvoc)
    ]
    whole = jnp.concatenate(pieces, axis=1)
    grad_trunk = whole[:tok]
    grad_residual = whole[tok : 2 * tok]
    grad_gain = whole[2 * tok].astype(f32) + whole[2 * tok + 1].astype(f32)
    return (grad_trunk, grad_residual, grad_gain, grad_head, grad_attn, grad_out_proj)


NT = (((1,), (1,)), ((), ()))
NN = (((1,), (0,)), ((), ()))


def iota(shape, dim):
    return lax.broadcasted_iota(jnp.int32, shape, dim)


def matmul(a, b, dims=NN):
    return lax.dot_general(a, b, dims, preferred_element_type=jnp.float32)


def onehot(mask):
    return jnp.where(mask, 1.0, 0.0).astype(jnp.bfloat16)


def chunks(width):
    step = next(s for s in (1024, 512, 256, 128) if width % s == 0)
    return [slice(c, c + step) for c in range(0, width, step)]


def kernel_call(body, outs, *args, side=None, away=()):
    vmem, hbm = pl.BlockSpec(memory_space=pltpu.VMEM), pl.BlockSpec(memory_space=pltpu.HBM)
    return pl.pallas_call(
        body,
        in_specs=[hbm if k in away else vmem for k in range(len(args))],
        out_specs=[vmem] * len(outs),
        out_shape=[jax.ShapeDtypeStruct(s, d) for s, d in outs],
        scratch_shapes=side or [],
        compiler_params=pltpu.CompilerParams(vmem_limit_bytes=16 << 20),
    )(*args)


def line_of(row, nchip):
    return (row % 2) * nchip + row // 2


def ordered(mine, theirs):
    first = lax.axis_index("rows") % 2 == 0
    return jnp.concatenate([jnp.where(first, mine, theirs), jnp.where(first, theirs, mine)], axis=0)


def head_kernel(tok, mine_ref, theirs_ref, w_ref, gain_ref, ids_ref, hid_ref, lt_ref, tgt_ref, inv_ref, msg_ref):
    f32, bf16 = jnp.float32, jnp.bfloat16
    half, width = mine_ref.shape
    rows, vrows = 2 * half, w_ref.shape[0]
    module = (iota((rows, 1), 0) // tok) % 2 == 1
    square = jnp.zeros((rows, 1), f32)
    for c in chunks(width):
        x = ordered(mine_ref[:, c].astype(f32), theirs_ref[:, c].astype(f32))
        square += jnp.sum(x * x, axis=1, keepdims=True)
    inverse = lax.rsqrt(square / width + norm_eps)
    inv_ref[...] = inverse
    lt = jnp.zeros((vrows, rows), f32)
    for c in chunks(width):
        x = ordered(mine_ref[:, c].astype(f32), theirs_ref[:, c].astype(f32))
        lines = slice(c.start // 128, c.stop // 128)
        gain = jnp.concatenate(
            [gain_ref[k : k + 1].astype(f32) for k in range(lines.start, lines.stop)], axis=1
        )
        h = jnp.where(module, x * inverse * gain, x).astype(bf16)
        hid_ref[:, c] = h
        lt += matmul(w_ref[:, c], h, NT)
    lt_ref[...] = lt
    eye = iota((half, half), 0) == iota((half, half), 1)
    main = jnp.sum(jnp.where(eye, ids_ref[:1], 0), axis=1, keepdims=True)
    other = jnp.sum(jnp.where(eye, ids_ref[1:], 0), axis=1, keepdims=True)
    src, dst = iota((half, rows), 0), iota((half, rows), 1)
    place = line_of(src // tok, half // tok // 2) * 2 * tok + src % tok
    tgt = jnp.where(dst == place, main, 0) + jnp.where(dst == place + tok, other, 0)
    tgt = jnp.sum(tgt, axis=0, keepdims=True)
    base = (lax.axis_index("vocab") * lax.axis_size("rows") + lax.axis_index("rows")) * vrows
    tgt = tgt - base
    tgt_ref[...] = tgt
    peak = jnp.max(lt, axis=0, keepdims=True)
    below = lt - peak
    weight = jnp.exp(below)
    picked = jnp.where(iota((vrows, rows), 0) == tgt, lt, 0.0)
    for k, stat in enumerate(
        (
            peak,
            jnp.sum(weight, axis=0, keepdims=True),
            jnp.sum(weight * below, axis=0, keepdims=True),
            jnp.sum(picked, axis=0, keepdims=True),
        )
    ):
        msg_ref[:, k * rows : (k + 1) * rows] = jnp.broadcast_to(stat, (msg_ref.shape[0], rows))


def loss_kernel(tok, cols, ev_ref, lt_ref, tgt_ref, w_ref, gt_ref, dot_ref, away_ref, keep_ref):
    f32, bf16 = jnp.float32, jnp.bfloat16
    vrows, rows = lt_ref.shape
    width = w_ref.shape[1]
    row, voc = lax.axis_index("rows"), lax.axis_index("vocab")
    core, chip = row % 2, row // 2
    peaks, masses, moments, picks = (ev_ref[:, k * rows : (k + 1) * rows] for k in range(4))
    top = jnp.max(peaks, axis=0, keepdims=True)
    drop = peaks - top
    factor = jnp.exp(drop)
    total = jnp.sum(factor * masses, axis=0, keepdims=True)
    spread = jnp.sum(factor * (moments + drop * masses), axis=0, keepdims=True) / total
    module = (iota((1, rows), 1) // tok) % 2 == 1
    share = jnp.where(module, loss_scale * mtp_share, loss_scale).astype(f32)
    dot_mean = share * (spread - (jnp.sum(picks, axis=0, keepdims=True) - top)) / width
    dot_mean = jnp.where(module, dot_mean, 0.0)
    eye = iota((rows, rows), 0) == iota((rows, rows), 1)
    dot_ref[...] = jnp.sum(jnp.where(eye, dot_mean, 0.0), axis=1, keepdims=True)
    hit = jnp.where(iota((vrows, rows), 0) == tgt_ref[...], 1.0, 0.0)
    gt = (share * (jnp.exp(lt_ref[...] - top) / total - hit)).astype(bf16)
    gt_ref[...] = gt
    line, col = iota((rows, rows), 0), iota((rows, rows), 1)
    half, quarter = rows // 2, rows // 4
    kind = line // half
    who = jnp.where((line % half) < quarter, core, 1 - core)
    spot = line % quarter
    owner = jnp.where(kind == 0, spot // tok, (spot // tok) ^ chip)
    want = (who * (quarter // tok) + owner) * 2 * tok + jnp.where(kind == 0, tok, 0) + spot % tok
    grads = matmul(onehot(col == want), gt, NT).astype(bf16)
    count = width // cols
    for k in range(count):
        total = matmul(grads, w_ref[:, k * cols : (k + 1) * cols]).astype(bf16)
        keep_ref[k ^ voc] = total[:quarter]
        away_ref[k ^ voc] = total[quarter:half]
        keep_ref[count + k] = total[half : half + quarter]
        away_ref[count + k] = total[half + quarter :]


def pair_kernel(nvoc, tok, keep_ref, got_ref, gt_ref, *outs):
    f32, bf16 = jnp.float32, jnp.bfloat16
    module, main, gt_out = outs[:nvoc], outs[nvoc:-1], outs[-1]
    gt_out[...] = gt_ref[...]
    for k, out in enumerate(module):
        out[...] = (keep_ref[k].astype(f32) + got_ref[k].astype(f32)).astype(bf16)
    cols = keep_ref.shape[2]
    for k in range(nvoc):
        total = keep_ref[nvoc + k].astype(f32) + got_ref[nvoc + k].astype(f32)
        for j, out in enumerate(main):
            out[:, k * cols : (k + 1) * cols] = total[j * tok : (j + 1) * tok].astype(bf16)


def column_kernel(nvoc, attn_ref, hold_ref, *refs):
    f32, bf16 = jnp.float32, jnp.bfloat16
    parts, outs = refs[:nvoc], refs[nvoc:]
    nmod, cols = parts[0].shape
    chip = lax.axis_index("rows") // 2
    total = tree_sum([p[...].astype(f32) for p in parts]).astype(bf16)
    tok, heads, size = attn_ref.shape
    each = heads // len(outs)
    line, spot = iota((each, heads), 0), iota((each, heads), 1)
    for j, out in enumerate(outs):
        out[:, :cols] = total
        pick = onehot(spot == (chip ^ j) * each + line)
        tail = jnp.concatenate([matmul(pick, attn_ref[i]) for i in range(tok)], axis=0)
        out[:, cols:] = tail.astype(bf16)


def main_kernel(*refs):
    for c in chunks(refs[-1].shape[1]):
        refs[-1][:, c] = tree_sum([m[:, c].astype(jnp.float32) for m in refs[:-1]]).astype(
            jnp.bfloat16
        )


def plane_kernel(tok, nchip, *refs):
    f32, bf16 = jnp.float32, jnp.bfloat16
    parts, (swap_ref, val_ref) = refs[:nchip], refs[nchip:]
    nmod, hdim = val_ref.shape
    size = parts[0].shape[1] - swap_ref.shape[1] + hdim
    cols = swap_ref.shape[1] - hdim
    each, heads = parts[0].shape[0] // tok, hdim // size
    swap_ref[:, :cols] = tree_sum([p[:, :cols].astype(f32) for p in parts]).astype(bf16)
    held = jnp.concatenate([p[:, cols:].astype(f32) for p in parts], axis=0).astype(bf16)
    core = lax.axis_index("rows") % 2
    line, spot = iota((nmod, held.shape[0]), 0), iota((nmod, held.shape[0]), 1)
    for h in range(heads):
        at = line * each + h
        lanes = slice(h * size, (h + 1) * size)
        val_ref[:, lanes] = matmul(onehot(spot == at + core * heads), held).astype(bf16)
        away = matmul(onehot(spot == at + (1 - core) * heads), held)
        swap_ref[:, cols + h * size : cols + (h + 1) * size] = away.astype(bf16)


def last_kernel(tok, mine_ref, theirs_ref, inv_ref, dot_ref, gain_ref, proj_ref, own_ref, other_ref, val_ref, res_ref, val_out, *outs):
    f32, bf16 = jnp.float32, jnp.bfloat16
    parcels, (scratch,) = outs[:-1], outs[-1:]
    half = mine_ref.shape[0]
    rows = 2 * half
    hdim, cols = proj_ref.shape
    nmod = own_ref.shape[0]
    nvoc = len(parcels)
    row, voc = lax.axis_index("rows"), lax.axis_index("vocab")
    core, chip = row % 2, row // 2
    nchip = nmod // tok
    line, spot = iota((rows, nmod), 0), iota((rows, nmod), 1)
    owner = line // (2 * tok)
    same = (line // tok) % 2 == 1
    same &= spot == (owner % nchip) * tok + line % tok
    grad = matmul(onehot(same & (owner // nchip == core)), own_ref[:, :cols])
    grad += matmul(onehot(same & (owner // nchip != core)), other_ref[:, :cols])
    start = pl.multiple_of(voc * cols, 128)
    inverse = inv_ref[...]
    at = pl.ds(start, cols)
    normed = ordered(mine_ref[:, at].astype(f32), theirs_ref[:, at].astype(f32)) * inverse
    gain_piece = jnp.sum(grad * normed, axis=0, keepdims=True)
    step = cols // 128
    gains = gain_ref[...].astype(f32)
    pick = iota(gains.shape, 0) - voc * step
    gain = jnp.concatenate(
        [jnp.sum(jnp.where(pick == k, gains, 0.0), axis=0, keepdims=True) for k in range(step)], axis=1
    )
    scaled = grad * gain
    wide = (inverse * (scaled - normed * dot_ref[...])).astype(bf16)
    line, spot = iota((half, rows), 0), iota((half, rows), 1)
    want = line_of(line // tok, nchip) * 2 * tok + tok + line % tok
    residual = matmul(onehot(spot == want), wide).astype(bf16)
    res_ref[...] = residual
    scratch[...] = matmul(residual, proj_ref[...], NT)
    tok_voc = half // nvoc
    fold = tok_voc // tok
    strip = cols // fold
    line, spot = iota((tok_voc, half), 0), iota((tok_voc, half), 1)
    mine = sum(
        matmul(
            onehot((line // tok == f) & (spot == row * tok + line % tok)),
            residual[:, f * strip : (f + 1) * strip],
        )
        for f in range(fold)
    ).astype(bf16)
    pieces = [gain_piece[:, c : c + hdim] for c in range(0, cols, hdim)]
    pieces += [jnp.zeros((1, hdim), f32)] * (tok_voc - len(pieces))
    gains = jnp.concatenate(pieces, axis=0)
    high = gains.astype(bf16)
    low = (gains - high.astype(f32)).astype(bf16)
    for k, out in enumerate(parcels):
        block = scratch[pl.ds(pl.multiple_of((voc ^ k) * tok_voc, tok_voc), tok_voc), :]
        out[:, :strip] = mine
        out[:, strip : strip + hdim] = block.astype(bf16)
        out[:, strip + hdim : strip + 2 * hdim] = high
        out[:, strip + 2 * hdim :] = low
    line, spot = iota((half, nmod), 0), iota((half, nmod), 1)
    owner = line // tok
    same = spot == ((owner // 2) ^ chip) * tok + line % tok
    values = matmul(onehot(same & (owner % 2 == core)), val_ref[...])
    values += matmul(onehot(same & (owner % 2 != core)), other_ref[:, cols:])
    val_out[...] = values.astype(bf16)


def proj_kernel(val_ref, res_ref, out_ref):
    out_ref[...] = matmul(val_ref[...], res_ref[...], (((0,), (0,)), ((), ()))).astype(out_ref.dtype)


def output_kernel(tok, nvoc, cols, *refs):
    f32, bf16 = jnp.float32, jnp.bfloat16
    parts, mains = refs[:nvoc], refs[nvoc : nvoc + 2]
    trunk_ref, res_ref, gain_ref, attn_ref = refs[nvoc + 2 :]
    count, heads, size = attn_ref.shape
    hdim = heads * size
    fold = count // tok
    strip = cols // fold
    voc = lax.axis_index("vocab")
    values = [p[...].astype(f32) for p in parts]
    for k, part in enumerate(values):
        for f in range(fold):
            at = pl.ds(pl.multiple_of((voc ^ k) * cols + f * strip, 128), strip)
            res_ref[:, at] = part[f * tok : (f + 1) * tok, :strip].astype(bf16)
        gains = part[:, strip + hdim : strip + 2 * hdim] + part[:, strip + 2 * hdim :]
        for i in range(cols // hdim):
            at = pl.ds(pl.multiple_of((voc ^ k) * cols + i * hdim, 128), hdim)
            gain_ref[:, at] = gains[i : i + 1]
    total = tree_sum([v[:, strip : strip + hdim] for v in values])
    for i in range(count):
        attn_ref[i] = jnp.concatenate(
            [total[i : i + 1, h * size : (h + 1) * size] for h in range(heads)], axis=0
        ).astype(bf16)
    for c in chunks(trunk_ref.shape[1]):
        trunk_ref[:, c] = tree_sum([m[:, c].astype(f32) for m in mains]).astype(bf16)


def local(
    trunk_hidden,
    mtp_state,
    mtp_gain,
    head_weight,
    target_ids,
    mtp_target_ids,
    attn_values,
    out_proj,
):
    f32, bf16 = jnp.float32, jnp.bfloat16
    tok, width = trunk_hidden.shape
    nrow = lax.axis_size("rows")
    nvoc = lax.axis_size("vocab")
    nchip = nrow // 2
    vrows = head_weight.shape[0]
    hdim, cols = out_proj.shape
    heads, size = attn_values.shape[1:]
    ntok = nrow * tok
    nmod = nchip * tok
    tok_voc = ntok // nvoc
    part = functools.partial

    gain = mtp_gain.reshape(width // 128, 128)
    ids = jnp.stack([target_ids, mtp_target_ids])
    stacked = jnp.concatenate([trunk_hidden, mtp_state], axis=0)
    mine = lax.all_gather(
        stacked,
        "rows",
        axis=0,
        tiled=True,
        axis_index_groups=[list(range(c, nrow, 2)) for c in range(2)],
    )
    theirs = swap(mine, "rows", 1)
    hidden, logits, targets, inverse, stats = kernel_call(
        part(head_kernel, tok),
        [
            ((2 * ntok, width), bf16),
            ((vrows, 2 * ntok), f32),
            ((1, 2 * ntok), jnp.int32),
            ((2 * ntok, 1), f32),
            ((nrow * nvoc, 8 * ntok), f32),
        ],
        mine,
        theirs,
        head_weight,
        gain,
        ids,
    )
    everyone = lax.all_to_all(
        stats, ("vocab", "rows"), split_axis=0, concat_axis=0, tiled=True
    )
    logit_grads, dot_mean, away, keep = kernel_call(
        part(loss_kernel, tok, cols),
        [
            ((vrows, 2 * ntok), bf16),
            ((2 * ntok, 1), f32),
            ((2 * nvoc, nmod, cols), bf16),
            ((2 * nvoc, nmod, cols), bf16),
        ],
        everyone,
        logits,
        targets,
        head_weight,
    )
    got = swap(away, "rows", 1)
    *pieces, logit_grads = kernel_call(
        part(pair_kernel, nvoc, tok),
        [((nmod, cols), bf16)] * nvoc
        + [((tok, width), bf16)] * nchip
        + [((vrows, 2 * ntok), bf16)],
        keep,
        got,
        logit_grads,
    )
    column, main = pieces[:nvoc], pieces[nvoc:]
    column = [column[0]] + [swap(column[k], "vocab", k) for k in range(1, nvoc)]
    main = [main[0]] + [swap(main[j], "rows", 2 * j) for j in range(1, nchip)]
    grad_head = lax.dot_general(
        logit_grads, hidden, (((1,), (0,)), ((), ())), preferred_element_type=f32
    ).astype(bf16)
    plane = kernel_call(
        part(column_kernel, nvoc),
        [((nmod, cols + size), bf16)] * nchip,
        attn_values,
        grad_head,
        *column,
        away=(1,),
    )
    plane = [plane[0]] + [swap(plane[j], "rows", 2 * j) for j in range(1, nchip)]
    (main,) = kernel_call(main_kernel, [((tok, width), bf16)], *main)
    near = swap(main, "vocab", 1)
    module, own_values = kernel_call(
        part(plane_kernel, tok, nchip),
        [((nmod, cols + hdim), bf16), ((nmod, hdim), bf16)],
        *plane,
    )
    (main,) = kernel_call(main_kernel, [((tok, width), bf16)], main, near)
    main = [main, swap(main, "vocab", 2)]
    other = swap(module, "rows", 1)
    residual, values, *parcels = kernel_call(
        part(last_kernel, tok),
        [((ntok, cols), bf16), ((ntok, hdim), bf16)]
        + [((tok_voc, cols * tok // tok_voc + 3 * hdim), bf16)] * nvoc,
        mine,
        theirs,
        inverse,
        dot_mean,
        gain,
        out_proj,
        module,
        other,
        own_values,
        side=[pltpu.VMEM((ntok, hdim), f32)],
    )
    parcels = [parcels[0]] + [swap(parcels[k], "vocab", k) for k in range(1, nvoc)]
    (grad_out_proj,) = kernel_call(proj_kernel, [((hdim, cols), bf16)], values, residual)
    grad_trunk, grad_residual, grad_gain, grad_attn = kernel_call(
        part(output_kernel, tok, nvoc, cols),
        [
            ((tok, width), bf16),
            ((tok, width), bf16),
            ((1, width), f32),
            ((tok_voc, hdim // size, size), bf16),
        ],
        *parcels,
        *main,
    )
    return (
        grad_trunk,
        grad_residual,
        grad_gain.reshape(width),
        grad_head,
        grad_attn,
        grad_out_proj,
    )


def choose(*args):
    tok, cols, hdim = args[0].shape[0], args[7].shape[1], args[7].shape[0]
    ntok = lax.axis_size("rows") * tok
    tok_voc = ntok // lax.axis_size("vocab")
    fits = (
        tok_voc == 8
        and lax.axis_size("vocab") == 4
        and tok_voc % tok == 0
        and cols % (128 * tok_voc // tok) == 0
        and hdim % 128 == 0
        and cols % hdim == 0
        and cols // hdim <= tok_voc
        and args[6].shape[1] // (lax.axis_size("rows") // 2) == tok
    )
    return local(*args) if fits else plain(*args)


def solution(mesh):
    return jax.shard_map(
        choose,
        mesh=mesh,
        in_specs=(
            P("rows", None),
            P("rows", None),
            P(),
            P(("vocab", "rows"), None),
            P(),
            P(),
            P("rows", None, None),
            P("rows", "vocab"),
        ),
        out_specs=(
            P("rows", None),
            P("rows", None),
            P(),
            P(("vocab", "rows"), None),
            P("vocab", "rows", None),
            P("rows", "vocab"),
        ),
        check_vma=False,
    )
```

```python
import functools

import jax
import jax.numpy as jnp
from jax import lax
from jax.experimental import pallas as pl
from jax.experimental.pallas import tpu as pltpu
from jax.sharding import PartitionSpec as P

loss_scale = 8.0
mtp_share = 0.3
norm_eps = 1e-06


def swap(x, axis, k):
    n = lax.axis_size(axis)
    return lax.ppermute(x, axis, [(i, i ^ k) for i in range(n)])


def tree_sum(parts):
    while len(parts) > 1:
        parts = [a + b for a, b in zip(parts[::2], parts[1::2])]
    return parts[0]


def plain(
    trunk_hidden,
    mtp_state,
    mtp_gain,
    head_weight,
    target_ids,
    mtp_target_ids,
    attn_values,
    out_proj,
):
    f32, bf16 = jnp.float32, jnp.bfloat16
    tok, width = trunk_hidden.shape
    nrow = lax.axis_size("rows")
    nvoc = lax.axis_size("vocab")
    ndev = nrow * nvoc
    nchip = nrow // 2
    row = lax.axis_index("rows")
    voc = lax.axis_index("vocab")
    core = row & 1
    chip = row >> 1
    vrows = head_weight.shape[0]
    cols = out_proj.shape[1]
    hdim = out_proj.shape[0]
    ntok = nrow * tok
    gain = mtp_gain.astype(f32)

    stacked = jnp.concatenate([trunk_hidden, mtp_state], axis=0)
    gathered = lax.all_gather(stacked, "rows", axis=0, tiled=True).reshape(nrow, 2, tok, width)
    state = gathered[:, 1].astype(f32)
    inverse = lax.rsqrt(jnp.mean(state * state, axis=-1, keepdims=True) + norm_eps)
    mtp_hidden = (state * inverse * gain).astype(bf16)
    hidden = jnp.stack([gathered[:, 0], mtp_hidden], axis=1).reshape(2 * ntok, width)

    targets = jnp.stack(
        [target_ids.reshape(nrow, tok), mtp_target_ids.reshape(nrow, tok)], axis=1
    ).reshape(-1)
    shares = jnp.broadcast_to(
        jnp.array([loss_scale, loss_scale * mtp_share], f32)[None, :, None], (nrow, 2, tok)
    ).reshape(-1)
    vocab_ids = (voc * nrow + row) * vrows + jnp.arange(vrows, dtype=jnp.int32)
    onehot = targets[:, None] == vocab_ids[None, :]

    logits = lax.dot_general(
        hidden, head_weight, (((1,), (1,)), ((), ())), preferred_element_type=f32
    )
    peak = jnp.max(logits, axis=1)
    below = logits - peak[:, None]
    weight = jnp.exp(below)
    mass = jnp.sum(weight, axis=1)
    moment = jnp.sum(weight * below, axis=1)
    picked = jnp.sum(jnp.where(onehot, logits, 0.0), axis=1)
    stats = jnp.stack([peak, mass, moment, picked])
    everyone = lax.all_to_all(
        jnp.broadcast_to(stats[None], (ndev,) + stats.shape),
        ("vocab", "rows"),
        split_axis=0,
        concat_axis=0,
        tiled=True,
    )
    peaks, masses, moments, picks = (everyone[:, k] for k in range(4))
    top = jnp.max(peaks, axis=0)
    drop = peaks - top
    factor = jnp.exp(drop)
    total = jnp.sum(factor * masses, axis=0)
    spread = jnp.sum(factor * (moments + drop * masses), axis=0) / total
    dot_mean = shares * (spread - (jnp.sum(picks, axis=0) - top)) / width
    dot_mean = dot_mean.reshape(nrow, 2, tok)[:, 1].reshape(ntok, 1)

    logit_grads = (
        shares[:, None] * (jnp.exp(logits - top[:, None]) / total[:, None] - onehot.astype(f32))
    ).astype(bf16)

    by_core = logit_grads.reshape(nchip, 2, 2, tok, vrows)

    def rows_for(which):
        part = lax.dynamic_index_in_dim(by_core, which, 1, keepdims=False)
        own = [lax.dynamic_index_in_dim(part, chip ^ j, 0, keepdims=False)[0] for j in range(nchip)]
        return jnp.concatenate([part[:, 1].reshape(nchip * tok, vrows)] + own, axis=0)

    def grads_of(rows):
        return jnp.dot(rows, head_weight, preferred_element_type=f32).astype(bf16)

    away = grads_of(rows_for(1 - core))
    kept = grads_of(rows_for(core))
    pair = (kept.astype(f32) + swap(away, "rows", 1).astype(f32)).astype(bf16)

    def columns_for(k):
        return lax.dynamic_slice_in_dim(pair, (voc ^ k) * cols, cols, 1)

    column_sum = tree_sum(
        [columns_for(0).astype(f32)]
        + [swap(columns_for(k), "vocab", k).astype(f32) for k in range(1, nvoc)]
    ).astype(bf16)
    nmod = nchip * tok
    module, main = column_sum[:nmod], column_sum[nmod:].reshape(nchip, tok, cols)
    plane = [jnp.concatenate([module, main[0]], axis=0)] + [
        swap(jnp.concatenate([module, main[j]], axis=0), "rows", 2 * j) for j in range(1, nchip)
    ]
    plane_sum = tree_sum([part.astype(f32) for part in plane]).astype(bf16)
    module, trunk_piece = plane_sum[:nmod], plane_sum[nmod:]
    other = swap(module, "rows", 1)

    grad_head = lax.dot_general(
        logit_grads, hidden, (((0,), (0,)), ((), ())), preferred_element_type=f32
    ).astype(bf16)
    values = lax.all_to_all(attn_values, "rows", split_axis=1, concat_axis=0, tiled=True)
    values = values.reshape(ntok, hdim)

    first = jnp.where(core == 0, module, other).reshape(nchip, 1, tok, cols)
    second = jnp.where(core == 0, other, module).reshape(nchip, 1, tok, cols)
    mtp_grad = jnp.concatenate([first, second], axis=1).reshape(ntok, cols).astype(f32)
    inv = inverse.reshape(ntok, 1)
    normed = lax.dynamic_slice_in_dim(
        gathered[:, 1].reshape(ntok, width), voc * cols, cols, 1
    ).astype(f32) * inv
    gain_piece = jnp.sum(mtp_grad * normed, axis=0, keepdims=True)
    scaled = mtp_grad * lax.dynamic_slice_in_dim(gain, voc * cols, cols, 0)
    residual = (inv * (scaled - normed * dot_mean)).astype(bf16)
    attn_terms = lax.dot_general(
        residual, out_proj, (((1,), (1,)), ((), ())), preferred_element_type=f32
    ).astype(bf16)
    grad_out_proj = lax.dot_general(
        values, residual, (((0,), (0,)), ((), ())), preferred_element_type=f32
    ).astype(bf16)

    residual_piece = lax.dynamic_slice_in_dim(residual, row * tok, tok, 0)
    gain_high = gain_piece.astype(bf16)
    gain_low = (gain_piece - gain_high.astype(f32)).astype(bf16)
    tok_voc = ntok // nvoc
    lines = -(-tok_voc * hdim // cols)
    terms = attn_terms.reshape(nvoc, tok_voc * hdim)
    terms = jnp.pad(terms, ((0, 0), (0, lines * cols - tok_voc * hdim))).reshape(nvoc, lines, cols)
    shared = jnp.concatenate([trunk_piece, residual_piece, gain_high, gain_low], axis=0)

    def parcel(k):
        mine = lax.dynamic_index_in_dim(terms, voc ^ k, 0, keepdims=False)
        return jnp.concatenate([shared, mine], axis=0)

    parcels = [parcel(0)] + [swap(parcel(k), "vocab", k) for k in range(1, nvoc)]
    ordered = jnp.stack(parcels)
    grad_attn = jnp.sum(ordered[:, 2 * tok + 2 :].astype(f32), axis=0).astype(bf16)
    grad_attn = grad_attn.reshape(-1)[: tok_voc * hdim].reshape(
        tok_voc, hdim // attn_values.shape[2], attn_values.shape[2]
    )
    pieces = [
        lax.dynamic_index_in_dim(ordered, voc ^ k, 0, keepdims=False)[: 2 * tok + 2]
        for k in range(nvoc)
    ]
    whole = jnp.concatenate(pieces, axis=1)
    grad_trunk = whole[:tok]
    grad_residual = whole[tok : 2 * tok]
    grad_gain = whole[2 * tok].astype(f32) + whole[2 * tok + 1].astype(f32)
    return (grad_trunk, grad_residual, grad_gain, grad_head, grad_attn, grad_out_proj)


NT = (((1,), (1,)), ((), ()))
NN = (((1,), (0,)), ((), ()))


def iota(shape, dim):
    return lax.broadcasted_iota(jnp.int32, shape, dim)


def matmul(a, b, dims=NN):
    return lax.dot_general(a, b, dims, preferred_element_type=jnp.float32)


def onehot(mask):
    return jnp.where(mask, 1.0, 0.0).astype(jnp.bfloat16)


def chunks(width):
    step = next(s for s in (1024, 512, 256, 128) if width % s == 0)
    return [slice(c, c + step) for c in range(0, width, step)]


def kernel_call(body, outs, *args, side=None, away=()):
    vmem, hbm = pl.BlockSpec(memory_space=pltpu.VMEM), pl.BlockSpec(memory_space=pltpu.HBM)
    return pl.pallas_call(
        body,
        in_specs=[hbm if k in away else vmem for k in range(len(args))],
        out_specs=[vmem] * len(outs),
        out_shape=[jax.ShapeDtypeStruct(s, d) for s, d in outs],
        scratch_shapes=side or [],
        compiler_params=pltpu.CompilerParams(vmem_limit_bytes=16 << 20),
    )(*args)


def line_of(row, nchip):
    return (row % 2) * nchip + row // 2


def module_lines(half, rows, tok):
    line, spot = iota((half, rows), 0), iota((half, rows), 1)
    return spot == line_of(line // tok, half // tok // 2) * 2 * tok + tok + line % tok


def ordered(mine, theirs):
    first = lax.axis_index("rows") % 2 == 0
    return jnp.concatenate([jnp.where(first, mine, theirs), jnp.where(first, theirs, mine)], axis=0)


def head_kernel(tok, mine_ref, theirs_ref, w_ref, gain_ref, ids_ref, hid_ref, lt_ref, tgt_ref, inv_ref, msg_ref):
    f32, bf16 = jnp.float32, jnp.bfloat16
    half, width = mine_ref.shape
    rows, vrows = 2 * half, w_ref.shape[0]
    module = (iota((rows, 1), 0) // tok) % 2 == 1
    square = jnp.zeros((rows, 1), f32)
    for c in chunks(width):
        x = ordered(mine_ref[:, c].astype(f32), theirs_ref[:, c].astype(f32))
        square += jnp.sum(x * x, axis=1, keepdims=True)
    inverse = lax.rsqrt(square / width + norm_eps)
    eye = iota((rows, rows), 0) == iota((rows, rows), 1)
    across = jnp.sum(jnp.where(eye, inverse, 0.0), axis=0, keepdims=True)
    pick = module_lines(half, rows, tok)
    inv_ref[...] = jnp.sum(jnp.where(pick, across, 0.0), axis=1, keepdims=True)
    lt = jnp.zeros((vrows, rows), f32)
    for c in chunks(width):
        x = ordered(mine_ref[:, c].astype(f32), theirs_ref[:, c].astype(f32))
        lines = slice(c.start // 128, c.stop // 128)
        gain = jnp.concatenate(
            [gain_ref[k : k + 1].astype(f32) for k in range(lines.start, lines.stop)], axis=1
        )
        h = jnp.where(module, x * inverse * gain, x).astype(bf16)
        hid_ref[:, c] = h
        lt += matmul(w_ref[:, c], h, NT)
    lt_ref[...] = lt
    eye = iota((half, half), 0) == iota((half, half), 1)
    main = jnp.sum(jnp.where(eye, ids_ref[:1], 0), axis=1, keepdims=True)
    other = jnp.sum(jnp.where(eye, ids_ref[1:], 0), axis=1, keepdims=True)
    src, dst = iota((half, rows), 0), iota((half, rows), 1)
    place = line_of(src // tok, half // tok // 2) * 2 * tok + src % tok
    tgt = jnp.where(dst == place, main, 0) + jnp.where(dst == place + tok, other, 0)
    tgt = jnp.sum(tgt, axis=0, keepdims=True)
    base = (lax.axis_index("vocab") * lax.axis_size("rows") + lax.axis_index("rows")) * vrows
    tgt = tgt - base
    tgt_ref[...] = tgt
    peak = jnp.max(lt, axis=0, keepdims=True)
    below = lt - peak
    weight = jnp.exp(below)
    picked = jnp.where(iota((vrows, rows), 0) == tgt, lt, 0.0)
    for k, stat in enumerate(
        (
            peak,
            jnp.sum(weight, axis=0, keepdims=True),
            jnp.sum(weight * below, axis=0, keepdims=True),
            jnp.sum(picked, axis=0, keepdims=True),
        )
    ):
        msg_ref[:, k * rows : (k + 1) * rows] = jnp.broadcast_to(stat, (msg_ref.shape[0], rows))


def loss_kernel(tok, cols, ev_ref, lt_ref, tgt_ref, w_ref, gt_ref, dot_ref, away_ref, keep_ref):
    f32, bf16 = jnp.float32, jnp.bfloat16
    vrows, rows = lt_ref.shape
    width = w_ref.shape[1]
    row, voc = lax.axis_index("rows"), lax.axis_index("vocab")
    core, chip = row % 2, row // 2
    peaks, masses, moments, picks = (ev_ref[:, k * rows : (k + 1) * rows] for k in range(4))
    top = jnp.max(peaks, axis=0, keepdims=True)
    drop = peaks - top
    factor = jnp.exp(drop)
    total = jnp.sum(factor * masses, axis=0, keepdims=True)
    spread = jnp.sum(factor * (moments + drop * masses), axis=0, keepdims=True) / total
    module = (iota((1, rows), 1) // tok) % 2 == 1
    share = jnp.where(module, loss_scale * mtp_share, loss_scale).astype(f32)
    dot_mean = share * (spread - (jnp.sum(picks, axis=0, keepdims=True) - top)) / width
    dot_ref[...] = jnp.sum(
        jnp.where(module_lines(rows // 2, rows, tok), dot_mean, 0.0), axis=1, keepdims=True
    )
    hit = jnp.where(iota((vrows, rows), 0) == tgt_ref[...], 1.0, 0.0)
    gt = (share * (jnp.exp(lt_ref[...] - top) / total - hit)).astype(bf16)
    gt_ref[...] = gt
    line, col = iota((rows, rows), 0), iota((rows, rows), 1)
    half, quarter = rows // 2, rows // 4
    kind = line // half
    who = jnp.where((line % half) < quarter, core, 1 - core)
    spot = line % quarter
    owner = jnp.where(kind == 0, spot // tok, (spot // tok) ^ chip)
    want = (who * (quarter // tok) + owner) * 2 * tok + jnp.where(kind == 0, tok, 0) + spot % tok
    grads = matmul(onehot(col == want), gt, NT).astype(bf16)
    count = width // cols
    for k in range(count):
        total = matmul(grads, w_ref[:, k * cols : (k + 1) * cols]).astype(bf16)
        keep_ref[k ^ voc] = total[:quarter]
        away_ref[k ^ voc] = total[quarter:half]
        keep_ref[count + k] = total[half : half + quarter]
        away_ref[count + k] = total[half + quarter :]


def pair_kernel(nvoc, tok, hold_ref, keep_ref, got_ref, *outs):
    f32, bf16 = jnp.float32, jnp.bfloat16
    module, main = outs[:nvoc], outs[nvoc:]
    for k, out in enumerate(module):
        out[...] = (keep_ref[k].astype(f32) + got_ref[k].astype(f32)).astype(bf16)
    cols = keep_ref.shape[2]
    for k in range(nvoc):
        total = keep_ref[nvoc + k].astype(f32) + got_ref[nvoc + k].astype(f32)
        for j, out in enumerate(main):
            out[:, k * cols : (k + 1) * cols] = total[j * tok : (j + 1) * tok].astype(bf16)


def column_kernel(nvoc, attn_ref, *refs):
    f32, bf16 = jnp.float32, jnp.bfloat16
    parts, outs = refs[:nvoc], refs[nvoc:]
    _, cols = parts[0].shape
    chip = lax.axis_index("rows") // 2
    total = tree_sum([p[...].astype(f32) for p in parts]).astype(bf16)
    tok, heads, _ = attn_ref.shape
    each = heads // len(outs)
    line, spot = iota((each, heads), 0), iota((each, heads), 1)
    for j, out in enumerate(outs):
        out[:, :cols] = total
        pick = onehot(spot == (chip ^ j) * each + line)
        tail = jnp.concatenate([matmul(pick, attn_ref[i]) for i in range(tok)], axis=0)
        out[:, cols:] = tail.astype(bf16)


def main_kernel(*refs):
    for c in chunks(refs[-1].shape[1]):
        refs[-1][:, c] = tree_sum([m[:, c].astype(jnp.float32) for m in refs[:-1]]).astype(
            jnp.bfloat16
        )


def plane_kernel(tok, nchip, *refs):
    f32, bf16 = jnp.float32, jnp.bfloat16
    parts, (swap_ref, val_ref) = refs[:nchip], refs[nchip:]
    nmod, hdim = val_ref.shape
    size = parts[0].shape[1] - swap_ref.shape[1] + hdim
    cols = swap_ref.shape[1] - hdim
    each, heads = parts[0].shape[0] // tok, hdim // size
    swap_ref[:, :cols] = tree_sum([p[:, :cols].astype(f32) for p in parts]).astype(bf16)
    held = jnp.concatenate([p[:, cols:].astype(f32) for p in parts], axis=0).astype(bf16)
    core = lax.axis_index("rows") % 2
    line, spot = iota((nmod, held.shape[0]), 0), iota((nmod, held.shape[0]), 1)
    for h in range(heads):
        at = line * each + h
        lanes = slice(h * size, (h + 1) * size)
        val_ref[:, lanes] = matmul(onehot(spot == at + core * heads), held).astype(bf16)
        away = matmul(onehot(spot == at + (1 - core) * heads), held)
        swap_ref[:, cols + h * size : cols + (h + 1) * size] = away.astype(bf16)


def last_kernel(tok, mine_ref, theirs_ref, inv_ref, dot_ref, gain_ref, proj_ref, own_ref, other_ref, val_ref, res_ref, val_out, *outs):
    f32, bf16 = jnp.float32, jnp.bfloat16
    parcels, (scratch,) = outs[:-1], outs[-1:]
    half = mine_ref.shape[0]
    rows = 2 * half
    hdim, cols = proj_ref.shape
    nmod = own_ref.shape[0]
    nvoc = len(parcels)
    row, voc = lax.axis_index("rows"), lax.axis_index("vocab")
    core, chip = row % 2, row // 2
    line, spot = iota((half, nmod), 0), iota((half, nmod), 1)
    owner = line // tok
    same = spot == (owner // 2) * tok + line % tok
    grad = matmul(onehot(same & (owner % 2 == core)), own_ref[:, :cols])
    grad += matmul(onehot(same & (owner % 2 != core)), other_ref[:, :cols])
    start = pl.multiple_of(voc * cols, 128)
    inverse = inv_ref[...]
    at = pl.ds(start, cols)
    state = ordered(mine_ref[:, at].astype(f32), theirs_ref[:, at].astype(f32)).astype(bf16)
    normed = matmul(onehot(module_lines(half, rows, tok)), state) * inverse
    gain_piece = jnp.sum(grad * normed, axis=0, keepdims=True)
    step = cols // 128
    gains = gain_ref[...].astype(f32)
    pick = iota(gains.shape, 0) - voc * step
    gain = jnp.concatenate(
        [jnp.sum(jnp.where(pick == k, gains, 0.0), axis=0, keepdims=True) for k in range(step)], axis=1
    )
    scaled = grad * gain
    residual = (inverse * (scaled - normed * dot_ref[...])).astype(bf16)
    res_ref[...] = residual
    scratch[...] = matmul(residual, proj_ref[...], NT)
    tok_voc = half // nvoc
    fold = tok_voc // tok
    strip = cols // fold
    line, spot = iota((tok_voc, half), 0), iota((tok_voc, half), 1)
    mine = sum(
        matmul(
            onehot((line // tok == f) & (spot == row * tok + line % tok)),
            residual[:, f * strip : (f + 1) * strip],
        )
        for f in range(fold)
    ).astype(bf16)
    pieces = [gain_piece[:, c : c + hdim] for c in range(0, cols, hdim)]
    pieces += [jnp.zeros((1, hdim), f32)] * (tok_voc - len(pieces))
    gains = jnp.concatenate(pieces, axis=0)
    high = gains.astype(bf16)
    low = (gains - high.astype(f32)).astype(bf16)
    for k, out in enumerate(parcels):
        block = scratch[pl.ds(pl.multiple_of((voc ^ k) * tok_voc, tok_voc), tok_voc), :]
        out[:, :strip] = mine
        out[:, strip : strip + hdim] = block.astype(bf16)
        out[:, strip + hdim : strip + 2 * hdim] = high
        out[:, strip + 2 * hdim :] = low
    line, spot = iota((half, nmod), 0), iota((half, nmod), 1)
    owner = line // tok
    same = spot == ((owner // 2) ^ chip) * tok + line % tok
    values = matmul(onehot(same & (owner % 2 == core)), val_ref[...])
    values += matmul(onehot(same & (owner % 2 != core)), other_ref[:, cols:])
    val_out[...] = values.astype(bf16)


def proj_kernel(val_ref, res_ref, out_ref):
    out_ref[...] = matmul(val_ref[...], res_ref[...], (((0,), (0,)), ((), ()))).astype(out_ref.dtype)


def output_kernel(tok, nvoc, cols, *refs):
    f32, bf16 = jnp.float32, jnp.bfloat16
    parts, mains = refs[:nvoc], refs[nvoc : nvoc + 2]
    trunk_ref, res_ref, gain_ref, attn_ref = refs[nvoc + 2 :]
    count, heads, size = attn_ref.shape
    hdim = heads * size
    fold = count // tok
    strip = cols // fold
    voc = lax.axis_index("vocab")
    values = [p[...].astype(f32) for p in parts]
    for k, part in enumerate(values):
        for f in range(fold):
            at = pl.ds(pl.multiple_of((voc ^ k) * cols + f * strip, 128), strip)
            res_ref[:, at] = part[f * tok : (f + 1) * tok, :strip].astype(bf16)
        gains = part[:, strip + hdim : strip + 2 * hdim] + part[:, strip + 2 * hdim :]
        for i in range(cols // hdim):
            at = pl.ds(pl.multiple_of((voc ^ k) * cols + i * hdim, 128), hdim)
            gain_ref[:, at] = gains[i : i + 1]
    total = tree_sum([v[:, strip : strip + hdim] for v in values])
    for i in range(count):
        attn_ref[i] = jnp.concatenate(
            [total[i : i + 1, h * size : (h + 1) * size] for h in range(heads)], axis=0
        ).astype(bf16)
    for c in chunks(trunk_ref.shape[1]):
        trunk_ref[:, c] = tree_sum([m[:, c].astype(f32) for m in mains]).astype(bf16)


def local(
    trunk_hidden,
    mtp_state,
    mtp_gain,
    head_weight,
    target_ids,
    mtp_target_ids,
    attn_values,
    out_proj,
):
    f32, bf16 = jnp.float32, jnp.bfloat16
    tok, width = trunk_hidden.shape
    nrow = lax.axis_size("rows")
    nvoc = lax.axis_size("vocab")
    nchip = nrow // 2
    vrows = head_weight.shape[0]
    hdim, cols = out_proj.shape
    _, size = attn_values.shape[1:]
    ntok = nrow * tok
    nmod = nchip * tok
    tok_voc = ntok // nvoc
    part = functools.partial

    gain = mtp_gain.reshape(width // 128, 128)
    ids = jnp.stack([target_ids, mtp_target_ids])
    stacked = jnp.concatenate([trunk_hidden, mtp_state], axis=0)
    mine = lax.all_gather(
        stacked,
        "rows",
        axis=0,
        tiled=True,
        axis_index_groups=[list(range(c, nrow, 2)) for c in range(2)],
    )
    theirs = swap(mine, "rows", 1)
    hidden, logits, targets, inverse, stats = kernel_call(
        part(head_kernel, tok),
        [
            ((2 * ntok, width), bf16),
            ((vrows, 2 * ntok), f32),
            ((1, 2 * ntok), jnp.int32),
            ((ntok, 1), f32),
            ((nrow * nvoc, 8 * ntok), f32),
        ],
        mine,
        theirs,
        head_weight,
        gain,
        ids,
    )
    everyone = lax.all_to_all(
        stats, ("vocab", "rows"), split_axis=0, concat_axis=0, tiled=True
    )
    logit_grads, dot_mean, away, keep = kernel_call(
        part(loss_kernel, tok, cols),
        [
            ((vrows, 2 * ntok), bf16),
            ((ntok, 1), f32),
            ((2 * nvoc, nmod, cols), bf16),
            ((2 * nvoc, nmod, cols), bf16),
        ],
        everyone,
        logits,
        targets,
        head_weight,
    )
    got = swap(away, "rows", 1)
    grad_head = lax.dot_general(
        logit_grads, hidden, (((1,), (0,)), ((), ())), preferred_element_type=f32
    ).astype(bf16)
    pieces = kernel_call(
        part(pair_kernel, nvoc, tok),
        [((nmod, cols), bf16)] * nvoc + [((tok, width), bf16)] * nchip,
        grad_head,
        keep,
        got,
        away=(0,),
    )
    column, main = pieces[:nvoc], pieces[nvoc:]
    column = swaps(column, "vocab", 1)
    main = swaps(main, "rows", 2)
    plane = kernel_call(
        part(column_kernel, nvoc),
        [((nmod, cols + size), bf16)] * nchip,
        attn_values,
        *column,
    )
    plane = swaps(plane, "rows", 2)
    (main,) = kernel_call(main_kernel, [((tok, width), bf16)], *main)
    near = swap(main, "vocab", 1)
    module, own_values = kernel_call(
        part(plane_kernel, tok, nchip),
        [((nmod, cols + hdim), bf16), ((nmod, hdim), bf16)],
        *plane,
    )
    (main,) = kernel_call(main_kernel, [((tok, width), bf16)], main, near)
    main = [main, swap(main, "vocab", 2)]
    other = swap(module, "rows", 1)
    residual, values, *parcels = kernel_call(
        part(last_kernel, tok),
        [((ntok, cols), bf16), ((ntok, hdim), bf16)]
        + [((tok_voc, cols * tok // tok_voc + 3 * hdim), bf16)] * nvoc,
        mine,
        theirs,
        inverse,
        dot_mean,
        gain,
        out_proj,
        module,
        other,
        own_values,
        side=[pltpu.VMEM((ntok, hdim), f32)],
    )
    parcels = swaps(parcels, "vocab", 1)
    (grad_out_proj,) = kernel_call(proj_kernel, [((hdim, cols), bf16)], values, residual)
    grad_trunk, grad_residual, grad_gain, grad_attn = kernel_call(
        part(output_kernel, tok, nvoc, cols),
        [
            ((tok, width), bf16),
            ((tok, width), bf16),
            ((1, width), f32),
            ((tok_voc, hdim // size, size), bf16),
        ],
        *parcels,
        *main,
    )
    return (
        grad_trunk,
        grad_residual,
        grad_gain.reshape(width),
        grad_head,
        grad_attn,
        grad_out_proj,
    )


def swaps(parts, axis, unit):
    got = [parts[0]]
    for k in range(1, len(parts)):
        got.append(swap(parts[k], axis, k * unit))
    return got


def choose(*args):
    tok, cols, hdim = args[0].shape[0], args[7].shape[1], args[7].shape[0]
    ntok = lax.axis_size("rows") * tok
    tok_voc = ntok // lax.axis_size("vocab")
    fits = (
        tok_voc == 8
        and lax.axis_size("vocab") == 4
        and tok_voc % tok == 0
        and cols % (128 * tok_voc // tok) == 0
        and hdim % 128 == 0
        and cols % hdim == 0
        and cols // hdim <= tok_voc
        and args[6].shape[1] // (lax.axis_size("rows") // 2) == tok
    )
    if not fits:
        return plain(*args)
    return local(*args)


def solution(mesh):
    return jax.shard_map(
        choose,
        mesh=mesh,
        in_specs=(
            P("rows", None),
            P("rows", None),
            P(),
            P(("vocab", "rows"), None),
            P(),
            P(),
            P("rows", None, None),
            P("rows", "vocab"),
        ),
        out_specs=(
            P("rows", None),
            P("rows", None),
            P(),
            P(("vocab", "rows"), None),
            P("vocab", "rows", None),
            P("rows", "vocab"),
        ),
        check_vma=False,
    )
```

```python
import functools

import jax
import jax.numpy as jnp
from jax import lax
from jax.experimental import pallas as pl
from jax.experimental.pallas import tpu as pltpu
from jax.sharding import PartitionSpec as P

loss_scale = 8.0
mtp_share = 0.3
norm_eps = 1e-06


def swap(x, axis, k):
    n = lax.axis_size(axis)
    return lax.ppermute(x, axis, [(i, i ^ k) for i in range(n)])


def tree_sum(parts):
    while len(parts) > 1:
        parts = [a + b for a, b in zip(parts[::2], parts[1::2])]
    return parts[0]


def plain(
    trunk_hidden,
    mtp_state,
    mtp_gain,
    head_weight,
    target_ids,
    mtp_target_ids,
    attn_values,
    out_proj,
):
    f32, bf16 = jnp.float32, jnp.bfloat16
    tok, width = trunk_hidden.shape
    nrow = lax.axis_size("rows")
    nvoc = lax.axis_size("vocab")
    ndev = nrow * nvoc
    nchip = nrow // 2
    row = lax.axis_index("rows")
    voc = lax.axis_index("vocab")
    core = row & 1
    chip = row >> 1
    vrows = head_weight.shape[0]
    cols = out_proj.shape[1]
    hdim = out_proj.shape[0]
    ntok = nrow * tok
    gain = mtp_gain.astype(f32)

    stacked = jnp.concatenate([trunk_hidden, mtp_state], axis=0)
    gathered = lax.all_gather(stacked, "rows", axis=0, tiled=True).reshape(nrow, 2, tok, width)
    state = gathered[:, 1].astype(f32)
    inverse = lax.rsqrt(jnp.mean(state * state, axis=-1, keepdims=True) + norm_eps)
    mtp_hidden = (state * inverse * gain).astype(bf16)
    hidden = jnp.stack([gathered[:, 0], mtp_hidden], axis=1).reshape(2 * ntok, width)

    targets = jnp.stack(
        [target_ids.reshape(nrow, tok), mtp_target_ids.reshape(nrow, tok)], axis=1
    ).reshape(-1)
    shares = jnp.broadcast_to(
        jnp.array([loss_scale, loss_scale * mtp_share], f32)[None, :, None], (nrow, 2, tok)
    ).reshape(-1)
    vocab_ids = (voc * nrow + row) * vrows + jnp.arange(vrows, dtype=jnp.int32)
    onehot = targets[:, None] == vocab_ids[None, :]

    logits = lax.dot_general(
        hidden, head_weight, (((1,), (1,)), ((), ())), preferred_element_type=f32
    )
    peak = jnp.max(logits, axis=1)
    below = logits - peak[:, None]
    weight = jnp.exp(below)
    mass = jnp.sum(weight, axis=1)
    moment = jnp.sum(weight * below, axis=1)
    picked = jnp.sum(jnp.where(onehot, logits, 0.0), axis=1)
    stats = jnp.stack([peak, mass, moment, picked])
    everyone = lax.all_to_all(
        jnp.broadcast_to(stats[None], (ndev,) + stats.shape),
        ("vocab", "rows"),
        split_axis=0,
        concat_axis=0,
        tiled=True,
    )
    peaks, masses, moments, picks = (everyone[:, k] for k in range(4))
    top = jnp.max(peaks, axis=0)
    drop = peaks - top
    factor = jnp.exp(drop)
    total = jnp.sum(factor * masses, axis=0)
    spread = jnp.sum(factor * (moments + drop * masses), axis=0) / total
    dot_mean = shares * (spread - (jnp.sum(picks, axis=0) - top)) / width
    dot_mean = dot_mean.reshape(nrow, 2, tok)[:, 1].reshape(ntok, 1)

    logit_grads = (
        shares[:, None] * (jnp.exp(logits - top[:, None]) / total[:, None] - onehot.astype(f32))
    ).astype(bf16)

    by_core = logit_grads.reshape(nchip, 2, 2, tok, vrows)

    def rows_for(which):
        part = lax.dynamic_index_in_dim(by_core, which, 1, keepdims=False)
        own = [lax.dynamic_index_in_dim(part, chip ^ j, 0, keepdims=False)[0] for j in range(nchip)]
        return jnp.concatenate([part[:, 1].reshape(nchip * tok, vrows)] + own, axis=0)

    def grads_of(rows):
        return jnp.dot(rows, head_weight, preferred_element_type=f32).astype(bf16)

    away = grads_of(rows_for(1 - core))
    kept = grads_of(rows_for(core))
    pair = (kept.astype(f32) + swap(away, "rows", 1).astype(f32)).astype(bf16)

    def columns_for(k):
        return lax.dynamic_slice_in_dim(pair, (voc ^ k) * cols, cols, 1)

    column_sum = tree_sum(
        [columns_for(0).astype(f32)]
        + [swap(columns_for(k), "vocab", k).astype(f32) for k in range(1, nvoc)]
    ).astype(bf16)
    nmod = nchip * tok
    module, main = column_sum[:nmod], column_sum[nmod:].reshape(nchip, tok, cols)
    plane = [jnp.concatenate([module, main[0]], axis=0)] + [
        swap(jnp.concatenate([module, main[j]], axis=0), "rows", 2 * j) for j in range(1, nchip)
    ]
    plane_sum = tree_sum([part.astype(f32) for part in plane]).astype(bf16)
    module, trunk_piece = plane_sum[:nmod], plane_sum[nmod:]
    other = swap(module, "rows", 1)

    grad_head = lax.dot_general(
        logit_grads, hidden, (((0,), (0,)), ((), ())), preferred_element_type=f32
    ).astype(bf16)
    values = lax.all_to_all(attn_values, "rows", split_axis=1, concat_axis=0, tiled=True)
    values = values.reshape(ntok, hdim)

    first = jnp.where(core == 0, module, other).reshape(nchip, 1, tok, cols)
    second = jnp.where(core == 0, other, module).reshape(nchip, 1, tok, cols)
    mtp_grad = jnp.concatenate([first, second], axis=1).reshape(ntok, cols).astype(f32)
    inv = inverse.reshape(ntok, 1)
    normed = lax.dynamic_slice_in_dim(
        gathered[:, 1].reshape(ntok, width), voc * cols, cols, 1
    ).astype(f32) * inv
    gain_piece = jnp.sum(mtp_grad * normed, axis=0, keepdims=True)
    scaled = mtp_grad * lax.dynamic_slice_in_dim(gain, voc * cols, cols, 0)
    residual = (inv * (scaled - normed * dot_mean)).astype(bf16)
    attn_terms = lax.dot_general(
        residual, out_proj, (((1,), (1,)), ((), ())), preferred_element_type=f32
    ).astype(bf16)
    grad_out_proj = lax.dot_general(
        values, residual, (((0,), (0,)), ((), ())), preferred_element_type=f32
    ).astype(bf16)

    residual_piece = lax.dynamic_slice_in_dim(residual, row * tok, tok, 0)
    gain_high = gain_piece.astype(bf16)
    gain_low = (gain_piece - gain_high.astype(f32)).astype(bf16)
    tok_voc = ntok // nvoc
    lines = -(-tok_voc * hdim // cols)
    terms = attn_terms.reshape(nvoc, tok_voc * hdim)
    terms = jnp.pad(terms, ((0, 0), (0, lines * cols - tok_voc * hdim))).reshape(nvoc, lines, cols)
    shared = jnp.concatenate([trunk_piece, residual_piece, gain_high, gain_low], axis=0)

    def parcel(k):
        mine = lax.dynamic_index_in_dim(terms, voc ^ k, 0, keepdims=False)
        return jnp.concatenate([shared, mine], axis=0)

    parcels = [parcel(0)] + [swap(parcel(k), "vocab", k) for k in range(1, nvoc)]
    ordered = jnp.stack(parcels)
    grad_attn = jnp.sum(ordered[:, 2 * tok + 2 :].astype(f32), axis=0).astype(bf16)
    grad_attn = grad_attn.reshape(-1)[: tok_voc * hdim].reshape(
        tok_voc, hdim // attn_values.shape[2], attn_values.shape[2]
    )
    pieces = [
        lax.dynamic_index_in_dim(ordered, voc ^ k, 0, keepdims=False)[: 2 * tok + 2]
        for k in range(nvoc)
    ]
    whole = jnp.concatenate(pieces, axis=1)
    grad_trunk = whole[:tok]
    grad_residual = whole[tok : 2 * tok]
    grad_gain = whole[2 * tok].astype(f32) + whole[2 * tok + 1].astype(f32)
    return (grad_trunk, grad_residual, grad_gain, grad_head, grad_attn, grad_out_proj)


NT = (((1,), (1,)), ((), ()))
NN = (((1,), (0,)), ((), ()))


def iota(shape, dim):
    return lax.broadcasted_iota(jnp.int32, shape, dim)


def matmul(a, b, dims=NN):
    return lax.dot_general(a, b, dims, preferred_element_type=jnp.float32)


def onehot(mask):
    return jnp.where(mask, 1.0, 0.0).astype(jnp.bfloat16)


def chunks(width):
    step = next(s for s in (1024, 512, 256, 128) if width % s == 0)
    return [slice(c, c + step) for c in range(0, width, step)]


def kernel_call(body, outs, *args, side=None, away=()):
    vmem, hbm = pl.BlockSpec(memory_space=pltpu.VMEM), pl.BlockSpec(memory_space=pltpu.HBM)
    return pl.pallas_call(
        body,
        in_specs=[hbm if k in away else vmem for k in range(len(args))],
        out_specs=[vmem] * len(outs),
        out_shape=[jax.ShapeDtypeStruct(s, d) for s, d in outs],
        scratch_shapes=side or [],
        compiler_params=pltpu.CompilerParams(vmem_limit_bytes=16 << 20),
    )(*args)


def module_lines(half, rows, tok):
    line, spot = iota((half, rows), 0), iota((half, rows), 1)
    owner = line // tok
    block = (owner % 2 ^ lax.axis_index("rows") % 2) * (half // tok // 2) + owner // 2
    return spot == block * 2 * tok + tok + line % tok


def in_order(near, tok, half):
    pick = module_lines(half, near.shape[1], tok)
    return jnp.sum(jnp.where(pick, near, 0.0), axis=1, keepdims=True)


def across(column):
    eye = iota((column.shape[0],) * 2, 0) == iota((column.shape[0],) * 2, 1)
    return jnp.sum(jnp.where(eye, column, 0.0), axis=0, keepdims=True)


def vocab_rows(vrows):
    row = lax.axis_index("rows")
    base = lax.axis_index("vocab") * lax.axis_size("rows")
    line = iota((2 * vrows, 1), 0)
    own = line < vrows
    return jnp.where(own, (base + row) * vrows + line, (base + (row ^ 1)) * vrows + line - vrows)


def prepare_kernel(tok, w_src, gain_src, ids_ref, mids_ref, w_ref, gain_ref, tgt_ref):
    f32 = jnp.float32
    w_ref[...] = w_src[...]
    gains = gain_src[...].astype(f32)
    for k in range(gains.shape[0]):
        gain_ref[:, k * 128 : (k + 1) * 128] = gains[k : k + 1]
    half, rows = ids_ref.shape[1], tgt_ref.shape[1]
    eye = iota((half, half), 0) == iota((half, half), 1)
    main = jnp.sum(jnp.where(eye, ids_ref[...], 0), axis=1, keepdims=True)
    other = jnp.sum(jnp.where(eye, mids_ref[...], 0), axis=1, keepdims=True)
    src, dst = iota((half, rows), 0), iota((half, rows), 1)
    own = src // tok % 2 == lax.axis_index("rows") % 2
    place = src // tok // 2 * 2 * tok + src % tok
    tgt = jnp.where(own & (dst == place), main, 0) + jnp.where(own & (dst == place + tok), other, 0)
    tgt_ref[...] = jnp.sum(tgt, axis=0, keepdims=True)


def inverse_of(x_ref, at):
    width = x_ref.shape[1]
    square = sum(jnp.square(x_ref[at, c].astype(jnp.float32)) for c in chunks(width))
    return lax.rsqrt(jnp.sum(square, axis=1, keepdims=True) / width + norm_eps)


def head_kernel(tok, count, *refs):
    f32, bf16 = jnp.float32, jnp.bfloat16
    blocks, (w_ref, part_ref, gain_ref, tgt_ref) = refs[:count], refs[count : count + 4]
    raw_ref, hid_ref, lt_ref, inv_ref, msg_ref = refs[count + 4 :]
    size, width = blocks[0].shape
    rows, vrows = count * size, w_ref.shape[0]
    chip = lax.axis_index("rows") // 2
    module = iota((size, 1), 0) // tok % 2 == 1
    inverses = [inverse_of(block, slice(None)) for block in blocks]
    places = [pl.ds(pl.multiple_of((chip ^ k) * size, size), size) for k in range(count)]
    for k in range(count):
        inv_ref[places[k]] = inverses[k]
    own = jnp.zeros((vrows, rows), f32)
    other = jnp.zeros((vrows, rows), f32)
    for c in chunks(width):
        gain = gain_ref[:, c]
        for k, block in enumerate(blocks):
            raw = block[:, c]
            x = raw.astype(f32)
            raw_ref[places[k], c] = raw
            hid_ref[places[k], c] = jnp.where(module, x * inverses[k] * gain, x).astype(bf16)
        h = hid_ref[:, c]
        own += matmul(w_ref[:, c], h, NT)
        other += matmul(part_ref[:, c], h, NT)
    lt = jnp.concatenate([own, other], axis=0)
    lt_ref[...] = lt
    peak = jnp.max(lt, axis=0, keepdims=True)
    below = lt - peak
    weight = jnp.exp(below)
    picked = jnp.where(vocab_rows(vrows) == tgt_ref[...], lt, 0.0)
    for k, stat in enumerate(
        (
            peak,
            jnp.sum(weight, axis=0, keepdims=True),
            jnp.sum(weight * below, axis=0, keepdims=True),
            jnp.sum(picked, axis=0, keepdims=True),
        )
    ):
        msg_ref[:, k * rows : (k + 1) * rows] = jnp.broadcast_to(stat, (msg_ref.shape[0], rows))


def loss_kernel(tok, nvoc, ev_ref, lt_ref, tgt_ref, w_ref, part_ref, own_ref, away_ref, dot_ref, *outs):
    f32, bf16 = jnp.float32, jnp.bfloat16
    vrows, width = w_ref.shape
    rows = lt_ref.shape[1]
    row, voc = lax.axis_index("rows"), lax.axis_index("vocab")
    core, chip = row % 2, row // 2
    module = (iota((1, rows), 1) // tok) % 2 == 1
    share = jnp.where(module, loss_scale * mtp_share, loss_scale).astype(f32)
    peaks, masses, moments, picks = (ev_ref[:, k * rows : (k + 1) * rows] for k in range(4))
    sender = iota((ev_ref.shape[0], 1), 0) % 2

    def combine(which):
        mine = sender == which
        top = jnp.max(jnp.where(mine, peaks, -jnp.inf), axis=0, keepdims=True)
        drop = jnp.where(mine, peaks - top, 0.0)
        factor = jnp.where(mine, jnp.exp(drop), 0.0)
        total = jnp.sum(factor * masses, axis=0, keepdims=True)
        spread = jnp.sum(factor * (moments + drop * masses), axis=0, keepdims=True) / total
        picked = jnp.sum(jnp.where(mine, picks, 0.0), axis=0, keepdims=True)
        return top, total, share * (spread - (picked - top)) / width

    top, total, dot_own = combine(core)
    dot_other = combine(1 - core)[2]
    dot_ref[...] = in_order(jnp.concatenate([dot_own, dot_other], axis=1), tok, dot_ref.shape[0])
    hit = jnp.where(vocab_rows(vrows) == tgt_ref[...], 1.0, 0.0)
    gt = (share * (jnp.exp(lt_ref[...] - top) / total - hit)).astype(bf16)
    own_ref[...] = gt[:vrows]
    away_ref[...] = gt[vrows:]
    column, main = outs[:nvoc], outs[nvoc:]
    half = rows // 2
    line, col = iota((rows, rows), 0), iota((rows, rows), 1)
    spot = line % half
    want = jnp.where(
        line < half, spot // tok * 2 * tok + tok, (spot // tok ^ chip) * 2 * tok
    )
    pick = onehot(col == want + spot % tok)
    grads = matmul(pick, gt[:vrows], NT).astype(bf16)
    others = matmul(pick, gt[vrows:], NT).astype(bf16)
    cols = width // nvoc
    for k in range(nvoc):
        at = pl.ds(pl.multiple_of((voc ^ k) * cols, 128), cols)
        total = matmul(grads, w_ref[:, at]) + matmul(others, part_ref[:, at])
        column[k][...] = total[:half].astype(bf16)
        for j, out in enumerate(main):
            out[:, at] = total[half + j * tok : half + (j + 1) * tok].astype(bf16)


def rest_kernel(tok, raw_ref, gain_ref, hid_ref, own_ref, got_ref, hid_out, gt_out, inv_out):
    f32, bf16 = jnp.float32, jnp.bfloat16
    rows, width = raw_ref.shape
    module = (iota((rows, 1), 0) // tok) % 2 == 1
    inverse = inverse_of(raw_ref, slice(None))
    inv_out[...] = inverse
    for c in chunks(width):
        x = raw_ref[:, c].astype(f32)
        hid_out[:rows, c] = hid_ref[:, c]
        hid_out[rows:, c] = jnp.where(module, x * inverse * gain_ref[:, c], x).astype(bf16)
    gt_out[:, :rows] = own_ref[...]
    gt_out[:, rows:] = got_ref[...]


def column_kernel(nvoc, attn_ref, *refs):
    f32, bf16 = jnp.float32, jnp.bfloat16
    parts, outs = refs[:nvoc], refs[nvoc:]
    _, cols = parts[0].shape
    chip = lax.axis_index("rows") // 2
    total = tree_sum([p[...].astype(f32) for p in parts]).astype(bf16)
    tok, heads, _ = attn_ref.shape
    each = heads // len(outs)
    line, spot = iota((each, heads), 0), iota((each, heads), 1)
    for j, out in enumerate(outs):
        out[:, :cols] = total
        pick = onehot(spot == (chip ^ j) * each + line)
        tail = jnp.concatenate([matmul(pick, attn_ref[i]) for i in range(tok)], axis=0)
        out[:, cols:] = tail.astype(bf16)


def main_kernel(*refs):
    for c in chunks(refs[-1].shape[1]):
        refs[-1][:, c] = tree_sum([m[:, c].astype(jnp.float32) for m in refs[:-1]]).astype(
            jnp.bfloat16
        )


def plane_kernel(tok, nchip, hold_ref, *refs):
    f32, bf16 = jnp.float32, jnp.bfloat16
    parts, (swap_ref, val_ref) = refs[:nchip], refs[nchip:]
    nmod, hdim = val_ref.shape
    size = parts[0].shape[1] - swap_ref.shape[1] + hdim
    cols = swap_ref.shape[1] - hdim
    each, heads = parts[0].shape[0] // tok, hdim // size
    swap_ref[:, :cols] = tree_sum([p[:, :cols].astype(f32) for p in parts]).astype(bf16)
    held = jnp.concatenate([p[:, cols:].astype(f32) for p in parts], axis=0).astype(bf16)
    core = lax.axis_index("rows") % 2
    line, spot = iota((nmod, held.shape[0]), 0), iota((nmod, held.shape[0]), 1)
    for h in range(heads):
        at = line * each + h
        lanes = slice(h * size, (h + 1) * size)
        val_ref[:, lanes] = matmul(onehot(spot == at + core * heads), held).astype(bf16)
        away = matmul(onehot(spot == at + (1 - core) * heads), held)
        swap_ref[:, cols + h * size : cols + (h + 1) * size] = away.astype(bf16)


def last_kernel(
    tok, raw_ref, part_ref, inv_ref, far_ref, dot_ref, gain_ref, proj_ref, own_ref, other_ref, val_ref, res_ref, val_out, *outs
):
    f32, bf16 = jnp.float32, jnp.bfloat16
    parcels, (scratch,) = outs[:-1], outs[-1:]
    half = raw_ref.shape[0]
    rows = 2 * half
    hdim, cols = proj_ref.shape
    nmod = own_ref.shape[0]
    nvoc = len(parcels)
    row, voc = lax.axis_index("rows"), lax.axis_index("vocab")
    core, chip = row % 2, row // 2
    line, spot = iota((half, nmod), 0), iota((half, nmod), 1)
    owner = line // tok
    same = spot == (owner // 2) * tok + line % tok
    grad = matmul(onehot(same & (owner % 2 == core)), own_ref[:, :cols])
    grad += matmul(onehot(same & (owner % 2 != core)), other_ref[:, :cols])
    start = pl.multiple_of(voc * cols, 128)
    near = jnp.concatenate([across(inv_ref[...]), across(far_ref[...])], axis=1)
    inverse = in_order(near, tok, half)
    at = pl.ds(start, cols)
    state = jnp.concatenate([raw_ref[:, at], part_ref[:, at]], axis=0)
    normed = matmul(onehot(module_lines(half, rows, tok)), state) * inverse
    gain_piece = jnp.sum(grad * normed, axis=0, keepdims=True)
    gain = gain_ref[:, pl.ds(start, cols)]
    scaled = grad * gain
    residual = (inverse * (scaled - normed * dot_ref[...])).astype(bf16)
    res_ref[...] = residual
    scratch[...] = matmul(residual, proj_ref[...], NT)
    tok_voc = half // nvoc
    fold = tok_voc // tok
    strip = cols // fold
    line, spot = iota((tok_voc, half), 0), iota((tok_voc, half), 1)
    mine = sum(
        matmul(
            onehot((line // tok == f) & (spot == row * tok + line % tok)),
            residual[:, f * strip : (f + 1) * strip],
        )
        for f in range(fold)
    ).astype(bf16)
    pieces = [gain_piece[:, c : c + hdim] for c in range(0, cols, hdim)]
    pieces += [jnp.zeros((1, hdim), f32)] * (tok_voc - len(pieces))
    gains = jnp.concatenate(pieces, axis=0)
    high = gains.astype(bf16)
    low = (gains - high.astype(f32)).astype(bf16)
    for k, out in enumerate(parcels):
        block = scratch[pl.ds(pl.multiple_of((voc ^ k) * tok_voc, tok_voc), tok_voc), :]
        out[:, :strip] = mine
        out[:, strip : strip + hdim] = block.astype(bf16)
        out[:, strip + hdim : strip + 2 * hdim] = high
        out[:, strip + 2 * hdim :] = low
    line, spot = iota((half, nmod), 0), iota((half, nmod), 1)
    owner = line // tok
    same = spot == ((owner // 2) ^ chip) * tok + line % tok
    values = matmul(onehot(same & (owner % 2 == core)), val_ref[...])
    values += matmul(onehot(same & (owner % 2 != core)), other_ref[:, cols:])
    val_out[...] = values.astype(bf16)


def proj_kernel(val_ref, res_ref, out_ref):
    out_ref[...] = matmul(val_ref[...], res_ref[...], (((0,), (0,)), ((), ()))).astype(out_ref.dtype)


def output_kernel(tok, nvoc, cols, *refs):
    f32, bf16 = jnp.float32, jnp.bfloat16
    parts, mains = refs[:nvoc], refs[nvoc : nvoc + 2]
    trunk_ref, res_ref, gain_ref, attn_ref = refs[nvoc + 2 :]
    count, heads, size = attn_ref.shape
    hdim = heads * size
    fold = count // tok
    strip = cols // fold
    voc = lax.axis_index("vocab")
    values = [p[...].astype(f32) for p in parts]
    for k, part in enumerate(values):
        for f in range(fold):
            at = pl.ds(pl.multiple_of((voc ^ k) * cols + f * strip, 128), strip)
            res_ref[:, at] = part[f * tok : (f + 1) * tok, :strip].astype(bf16)
        gains = part[:, strip + hdim : strip + 2 * hdim] + part[:, strip + 2 * hdim :]
        for i in range(cols // hdim):
            at = pl.ds(pl.multiple_of((voc ^ k) * cols + i * hdim, 128), hdim)
            gain_ref[:, at] = gains[i : i + 1]
    total = tree_sum([v[:, strip : strip + hdim] for v in values])
    for i in range(count):
        attn_ref[i] = jnp.concatenate(
            [total[i : i + 1, h * size : (h + 1) * size] for h in range(heads)], axis=0
        ).astype(bf16)
    for c in chunks(trunk_ref.shape[1]):
        trunk_ref[:, c] = tree_sum([m[:, c].astype(f32) for m in mains]).astype(bf16)


def local(
    trunk_hidden,
    mtp_state,
    mtp_gain,
    head_weight,
    target_ids,
    mtp_target_ids,
    attn_values,
    out_proj,
):
    f32, bf16 = jnp.float32, jnp.bfloat16
    tok, width = trunk_hidden.shape
    nrow = lax.axis_size("rows")
    nvoc = lax.axis_size("vocab")
    nchip = nrow // 2
    vrows = head_weight.shape[0]
    hdim, cols = out_proj.shape
    _, size = attn_values.shape[1:]
    ntok = nrow * tok
    nmod = nchip * tok
    tok_voc = ntok // nvoc
    part = functools.partial

    stacked = jnp.concatenate([trunk_hidden, mtp_state], axis=0)
    blocks = swaps([stacked] * nchip, "rows", 2)
    weight_near = swap(head_weight, "rows", 1)
    weight, gain, targets = kernel_call(
        part(prepare_kernel, tok),
        [((vrows, width), bf16), ((1, width), f32), ((1, ntok), jnp.int32)],
        head_weight,
        mtp_gain.reshape(width // 128, 128),
        target_ids.reshape(1, ntok),
        mtp_target_ids.reshape(1, ntok),
    )
    raw, hidden, logits, inverse, stats = kernel_call(
        part(head_kernel, tok, nchip),
        [
            ((ntok, width), bf16),
            ((ntok, width), bf16),
            ((2 * vrows, ntok), f32),
            ((ntok, 1), f32),
            ((nrow * nvoc, 4 * ntok), f32),
        ],
        *blocks,
        weight,
        weight_near,
        gain,
        targets,
    )
    raw_near = swap(raw, "rows", 1)
    everyone = lax.all_to_all(
        stats, ("vocab", "rows"), split_axis=0, concat_axis=0, tiled=True
    )
    grads, grads_away, dot_mean, *pieces = kernel_call(
        part(loss_kernel, tok, nvoc),
        [((vrows, ntok), bf16)] * 2
        + [((ntok, 1), f32)]
        + [((nmod, cols), bf16)] * nvoc
        + [((tok, width), bf16)] * nchip,
        everyone,
        logits,
        targets,
        weight,
        weight_near,
    )
    column, main = pieces[:nvoc], pieces[nvoc:]
    column = swaps(column, "vocab", 1)
    main = swaps(main, "rows", 2)
    grads_near = swap(grads_away, "rows", 1)
    hidden, logit_grads, inverse_near = kernel_call(
        part(rest_kernel, tok),
        [((2 * ntok, width), bf16), ((vrows, 2 * ntok), bf16), ((ntok, 1), f32)],
        raw_near,
        gain,
        hidden,
        grads,
        grads_near,
    )
    grad_head = lax.dot_general(
        logit_grads, hidden, (((1,), (0,)), ((), ())), preferred_element_type=f32
    ).astype(bf16)
    plane = kernel_call(
        part(column_kernel, nvoc),
        [((nmod, cols + size), bf16)] * nchip,
        attn_values,
        *column,
    )
    plane = swaps(plane, "rows", 2)
    (main,) = kernel_call(main_kernel, [((tok, width), bf16)], *main)
    near = swap(main, "vocab", 1)
    module, own_values = kernel_call(
        part(plane_kernel, tok, nchip),
        [((nmod, cols + hdim), bf16), ((nmod, hdim), bf16)],
        grad_head,
        *plane,
        away=(0,),
    )
    (main,) = kernel_call(main_kernel, [((tok, width), bf16)], main, near)
    main = [main, swap(main, "vocab", 2)]
    other = swap(module, "rows", 1)
    residual, values, *parcels = kernel_call(
        part(last_kernel, tok),
        [((ntok, cols), bf16), ((ntok, hdim), bf16)]
        + [((tok_voc, cols * tok // tok_voc + 3 * hdim), bf16)] * nvoc,
        raw,
        raw_near,
        inverse,
        inverse_near,
        dot_mean,
        gain,
        out_proj,
        module,
        other,
        own_values,
        side=[pltpu.VMEM((ntok, hdim), f32)],
    )
    parcels = swaps(parcels, "vocab", 1)
    (grad_out_proj,) = kernel_call(proj_kernel, [((hdim, cols), bf16)], values, residual)
    grad_trunk, grad_residual, grad_gain, grad_attn = kernel_call(
        part(output_kernel, tok, nvoc, cols),
        [
            ((tok, width), bf16),
            ((tok, width), bf16),
            ((1, width), f32),
            ((tok_voc, hdim // size, size), bf16),
        ],
        *parcels,
        *main,
    )
    return (
        grad_trunk,
        grad_residual,
        grad_gain.reshape(width),
        grad_head,
        grad_attn,
        grad_out_proj,
    )


def swaps(parts, axis, unit):
    got = [parts[0]]
    for k in range(1, len(parts)):
        got.append(swap(parts[k], axis, k * unit))
    return got


def choose(*args):
    tok, cols, hdim = args[0].shape[0], args[7].shape[1], args[7].shape[0]
    ntok = lax.axis_size("rows") * tok
    tok_voc = ntok // lax.axis_size("vocab")
    fits = (
        lax.axis_size("rows") == 8
        and ntok == 32
        and         tok_voc == 8
        and lax.axis_size("vocab") == 4
        and tok_voc % tok == 0
        and cols % (128 * tok_voc // tok) == 0
        and hdim % 128 == 0
        and cols % hdim == 0
        and cols // hdim <= tok_voc
        and args[6].shape[1] // (lax.axis_size("rows") // 2) == tok
    )
    if not fits:
        return plain(*args)
    return local(*args)


def solution(mesh):
    return jax.shard_map(
        choose,
        mesh=mesh,
        in_specs=(
            P("rows", None),
            P("rows", None),
            P(),
            P(("vocab", "rows"), None),
            P(),
            P(),
            P("rows", None, None),
            P("rows", "vocab"),
        ),
        out_specs=(
            P("rows", None),
            P("rows", None),
            P(),
            P(("vocab", "rows"), None),
            P("vocab", "rows", None),
            P("rows", "vocab"),
        ),
        check_vma=False,
    )
```

```python
import functools

import jax
import jax.numpy as jnp
from jax import lax
from jax.experimental import pallas as pl
from jax.experimental.pallas import tpu as pltpu
from jax.sharding import PartitionSpec as P

loss_scale = 8.0
mtp_share = 0.3
norm_eps = 1e-06


def swap(x, axis, k):
    n = lax.axis_size(axis)
    return lax.ppermute(x, axis, [(i, i ^ k) for i in range(n)])


def tree_sum(parts):
    while len(parts) > 1:
        parts = [a + b for a, b in zip(parts[::2], parts[1::2])]
    return parts[0]


def plain(
    trunk_hidden,
    mtp_state,
    mtp_gain,
    head_weight,
    target_ids,
    mtp_target_ids,
    attn_values,
    out_proj,
):
    f32, bf16 = jnp.float32, jnp.bfloat16
    tok, width = trunk_hidden.shape
    nrow = lax.axis_size("rows")
    nvoc = lax.axis_size("vocab")
    ndev = nrow * nvoc
    nchip = nrow // 2
    row = lax.axis_index("rows")
    voc = lax.axis_index("vocab")
    core = row & 1
    chip = row >> 1
    vrows = head_weight.shape[0]
    cols = out_proj.shape[1]
    hdim = out_proj.shape[0]
    ntok = nrow * tok
    gain = mtp_gain.astype(f32)

    stacked = jnp.concatenate([trunk_hidden, mtp_state], axis=0)
    gathered = lax.all_gather(stacked, "rows", axis=0, tiled=True).reshape(nrow, 2, tok, width)
    state = gathered[:, 1].astype(f32)
    inverse = lax.rsqrt(jnp.mean(state * state, axis=-1, keepdims=True) + norm_eps)
    mtp_hidden = (state * inverse * gain).astype(bf16)
    hidden = jnp.stack([gathered[:, 0], mtp_hidden], axis=1).reshape(2 * ntok, width)

    targets = jnp.stack(
        [target_ids.reshape(nrow, tok), mtp_target_ids.reshape(nrow, tok)], axis=1
    ).reshape(-1)
    shares = jnp.broadcast_to(
        jnp.array([loss_scale, loss_scale * mtp_share], f32)[None, :, None], (nrow, 2, tok)
    ).reshape(-1)
    vocab_ids = (voc * nrow + row) * vrows + jnp.arange(vrows, dtype=jnp.int32)
    onehot = targets[:, None] == vocab_ids[None, :]

    logits = lax.dot_general(
        hidden, head_weight, (((1,), (1,)), ((), ())), preferred_element_type=f32
    )
    peak = jnp.max(logits, axis=1)
    below = logits - peak[:, None]
    weight = jnp.exp(below)
    mass = jnp.sum(weight, axis=1)
    moment = jnp.sum(weight * below, axis=1)
    picked = jnp.sum(jnp.where(onehot, logits, 0.0), axis=1)
    stats = jnp.stack([peak, mass, moment, picked])
    everyone = lax.all_to_all(
        jnp.broadcast_to(stats[None], (ndev,) + stats.shape),
        ("vocab", "rows"),
        split_axis=0,
        concat_axis=0,
        tiled=True,
    )
    peaks, masses, moments, picks = (everyone[:, k] for k in range(4))
    top = jnp.max(peaks, axis=0)
    drop = peaks - top
    factor = jnp.exp(drop)
    total = jnp.sum(factor * masses, axis=0)
    spread = jnp.sum(factor * (moments + drop * masses), axis=0) / total
    dot_mean = shares * (spread - (jnp.sum(picks, axis=0) - top)) / width
    dot_mean = dot_mean.reshape(nrow, 2, tok)[:, 1].reshape(ntok, 1)

    logit_grads = (
        shares[:, None] * (jnp.exp(logits - top[:, None]) / total[:, None] - onehot.astype(f32))
    ).astype(bf16)

    by_core = logit_grads.reshape(nchip, 2, 2, tok, vrows)

    def rows_for(which):
        part = lax.dynamic_index_in_dim(by_core, which, 1, keepdims=False)
        own = [lax.dynamic_index_in_dim(part, chip ^ j, 0, keepdims=False)[0] for j in range(nchip)]
        return jnp.concatenate([part[:, 1].reshape(nchip * tok, vrows)] + own, axis=0)

    def grads_of(rows):
        return jnp.dot(rows, head_weight, preferred_element_type=f32).astype(bf16)

    away = grads_of(rows_for(1 - core))
    kept = grads_of(rows_for(core))
    pair = (kept.astype(f32) + swap(away, "rows", 1).astype(f32)).astype(bf16)

    def columns_for(k):
        return lax.dynamic_slice_in_dim(pair, (voc ^ k) * cols, cols, 1)

    column_sum = tree_sum(
        [columns_for(0).astype(f32)]
        + [swap(columns_for(k), "vocab", k).astype(f32) for k in range(1, nvoc)]
    ).astype(bf16)
    nmod = nchip * tok
    module, main = column_sum[:nmod], column_sum[nmod:].reshape(nchip, tok, cols)
    plane = [jnp.concatenate([module, main[0]], axis=0)] + [
        swap(jnp.concatenate([module, main[j]], axis=0), "rows", 2 * j) for j in range(1, nchip)
    ]
    plane_sum = tree_sum([part.astype(f32) for part in plane]).astype(bf16)
    module, trunk_piece = plane_sum[:nmod], plane_sum[nmod:]
    other = swap(module, "rows", 1)

    grad_head = lax.dot_general(
        logit_grads, hidden, (((0,), (0,)), ((), ())), preferred_element_type=f32
    ).astype(bf16)
    values = lax.all_to_all(attn_values, "rows", split_axis=1, concat_axis=0, tiled=True)
    values = values.reshape(ntok, hdim)

    first = jnp.where(core == 0, module, other).reshape(nchip, 1, tok, cols)
    second = jnp.where(core == 0, other, module).reshape(nchip, 1, tok, cols)
    mtp_grad = jnp.concatenate([first, second], axis=1).reshape(ntok, cols).astype(f32)
    inv = inverse.reshape(ntok, 1)
    normed = lax.dynamic_slice_in_dim(
        gathered[:, 1].reshape(ntok, width), voc * cols, cols, 1
    ).astype(f32) * inv
    gain_piece = jnp.sum(mtp_grad * normed, axis=0, keepdims=True)
    scaled = mtp_grad * lax.dynamic_slice_in_dim(gain, voc * cols, cols, 0)
    residual = (inv * (scaled - normed * dot_mean)).astype(bf16)
    attn_terms = lax.dot_general(
        residual, out_proj, (((1,), (1,)), ((), ())), preferred_element_type=f32
    ).astype(bf16)
    grad_out_proj = lax.dot_general(
        values, residual, (((0,), (0,)), ((), ())), preferred_element_type=f32
    ).astype(bf16)

    residual_piece = lax.dynamic_slice_in_dim(residual, row * tok, tok, 0)
    gain_high = gain_piece.astype(bf16)
    gain_low = (gain_piece - gain_high.astype(f32)).astype(bf16)
    tok_voc = ntok // nvoc
    lines = -(-tok_voc * hdim // cols)
    terms = attn_terms.reshape(nvoc, tok_voc * hdim)
    terms = jnp.pad(terms, ((0, 0), (0, lines * cols - tok_voc * hdim))).reshape(nvoc, lines, cols)
    shared = jnp.concatenate([trunk_piece, residual_piece, gain_high, gain_low], axis=0)

    def parcel(k):
        mine = lax.dynamic_index_in_dim(terms, voc ^ k, 0, keepdims=False)
        return jnp.concatenate([shared, mine], axis=0)

    parcels = [parcel(0)] + [swap(parcel(k), "vocab", k) for k in range(1, nvoc)]
    ordered = jnp.stack(parcels)
    grad_attn = jnp.sum(ordered[:, 2 * tok + 2 :].astype(f32), axis=0).astype(bf16)
    grad_attn = grad_attn.reshape(-1)[: tok_voc * hdim].reshape(
        tok_voc, hdim // attn_values.shape[2], attn_values.shape[2]
    )
    pieces = [
        lax.dynamic_index_in_dim(ordered, voc ^ k, 0, keepdims=False)[: 2 * tok + 2]
        for k in range(nvoc)
    ]
    whole = jnp.concatenate(pieces, axis=1)
    grad_trunk = whole[:tok]
    grad_residual = whole[tok : 2 * tok]
    grad_gain = whole[2 * tok].astype(f32) + whole[2 * tok + 1].astype(f32)
    return (grad_trunk, grad_residual, grad_gain, grad_head, grad_attn, grad_out_proj)


NT = (((1,), (1,)), ((), ()))
NN = (((1,), (0,)), ((), ()))


def iota(shape, dim):
    return lax.broadcasted_iota(jnp.int32, shape, dim)


def matmul(a, b, dims=NN):
    return lax.dot_general(a, b, dims, preferred_element_type=jnp.float32)


def onehot(mask):
    return jnp.where(mask, 1.0, 0.0).astype(jnp.bfloat16)


def chunks(width):
    step = next(s for s in (1024, 512, 256, 128) if width % s == 0)
    return [slice(c, c + step) for c in range(0, width, step)]


def kernel_call(body, outs, *args, side=None, away=()):
    vmem, hbm = pl.BlockSpec(memory_space=pltpu.VMEM), pl.BlockSpec(memory_space=pltpu.HBM)
    return pl.pallas_call(
        body,
        in_specs=[hbm if k in away else vmem for k in range(len(args))],
        out_specs=[vmem] * len(outs),
        out_shape=[jax.ShapeDtypeStruct(s, d) for s, d in outs],
        scratch_shapes=side or [],
        compiler_params=pltpu.CompilerParams(vmem_limit_bytes=16 << 20),
    )(*args)


def module_lines(half, rows, tok):
    line, spot = iota((half, rows), 0), iota((half, rows), 1)
    owner = line // tok
    block = (owner % 2 ^ lax.axis_index("rows") % 2) * (half // tok // 2) + owner // 2
    return spot == block * 2 * tok + tok + line % tok


def in_order(near, tok, half):
    pick = module_lines(half, near.shape[1], tok)
    return jnp.sum(jnp.where(pick, near, 0.0), axis=1, keepdims=True)


def across(column):
    eye = iota((column.shape[0],) * 2, 0) == iota((column.shape[0],) * 2, 1)
    return jnp.sum(jnp.where(eye, column, 0.0), axis=0, keepdims=True)


def vocab_rows(vrows):
    row = lax.axis_index("rows")
    base = lax.axis_index("vocab") * lax.axis_size("rows")
    line = iota((2 * vrows, 1), 0)
    own = line < vrows
    return jnp.where(own, (base + row) * vrows + line, (base + (row ^ 1)) * vrows + line - vrows)


def prepare_kernel(tok, w_src, gain_src, ids_ref, mids_ref, w_ref, gain_ref, tgt_ref):
    f32 = jnp.float32
    w_ref[...] = w_src[...]
    gains = gain_src[...].astype(f32)
    for k in range(gains.shape[0]):
        gain_ref[:, k * 128 : (k + 1) * 128] = gains[k : k + 1]
    half, rows = ids_ref.shape[1], tgt_ref.shape[1]
    eye = iota((half, half), 0) == iota((half, half), 1)
    main = jnp.sum(jnp.where(eye, ids_ref[...], 0), axis=1, keepdims=True)
    other = jnp.sum(jnp.where(eye, mids_ref[...], 0), axis=1, keepdims=True)
    src, dst = iota((half, rows), 0), iota((half, rows), 1)
    own = src // tok % 2 == lax.axis_index("rows") % 2
    place = src // tok // 2 * 2 * tok + src % tok
    tgt = jnp.where(own & (dst == place), main, 0) + jnp.where(own & (dst == place + tok), other, 0)
    tgt_ref[...] = jnp.sum(tgt, axis=0, keepdims=True)


def inverse_of(x_ref, at):
    width = x_ref.shape[1]
    square = sum(jnp.square(x_ref[at, c].astype(jnp.float32)) for c in chunks(width))
    return lax.rsqrt(jnp.sum(square, axis=1, keepdims=True) / width + norm_eps)


def head_kernel(tok, count, *refs):
    f32, bf16 = jnp.float32, jnp.bfloat16
    blocks, (w_ref, part_ref, gain_ref, tgt_ref) = refs[:count], refs[count : count + 4]
    raw_ref, hid_ref, lt_ref, inv_ref, msg_ref = refs[count + 4 :]
    size, width = blocks[0].shape
    rows, vrows = count * size, w_ref.shape[0]
    chip = lax.axis_index("rows") // 2
    module = iota((size, 1), 0) // tok % 2 == 1
    inverses = [inverse_of(block, slice(None)) for block in blocks]
    places = [pl.ds(pl.multiple_of((chip ^ k) * size, size), size) for k in range(count)]
    for k in range(count):
        inv_ref[places[k]] = inverses[k]
    own = jnp.zeros((vrows, rows), f32)
    other = jnp.zeros((vrows, rows), f32)
    for c in chunks(width):
        gain = gain_ref[:, c]
        for k, block in enumerate(blocks):
            raw = block[:, c]
            x = raw.astype(f32)
            raw_ref[places[k], c] = raw
            hid_ref[places[k], c] = jnp.where(module, x * inverses[k] * gain, x).astype(bf16)
        h = hid_ref[:, c]
        own += matmul(w_ref[:, c], h, NT)
        other += matmul(part_ref[:, c], h, NT)
    lt = jnp.concatenate([own, other], axis=0)
    lt_ref[...] = lt
    left, tail = inv_ref[...], jnp.zeros((rows, 128), f32)
    for k in range(3):
        term = left.astype(bf16).astype(f32)
        tail = jnp.where(iota(tail.shape, 1) == k, term, tail)
        left = left - term
    raw_ref[:, width:] = tail.astype(bf16)
    peak = jnp.max(lt, axis=0, keepdims=True)
    below = lt - peak
    weight = jnp.exp(below)
    picked = jnp.where(vocab_rows(vrows) == tgt_ref[...], lt, 0.0)
    for k, stat in enumerate(
        (
            peak,
            jnp.sum(weight, axis=0, keepdims=True),
            jnp.sum(weight * below, axis=0, keepdims=True),
            jnp.sum(picked, axis=0, keepdims=True),
        )
    ):
        msg_ref[:, k * rows : (k + 1) * rows] = jnp.broadcast_to(stat, (msg_ref.shape[0], rows))


def loss_kernel(tok, nvoc, ev_ref, lt_ref, tgt_ref, w_ref, part_ref, own_ref, away_ref, dot_ref, *outs):
    f32, bf16 = jnp.float32, jnp.bfloat16
    vrows, width = w_ref.shape
    rows = lt_ref.shape[1]
    row, voc = lax.axis_index("rows"), lax.axis_index("vocab")
    core, chip = row % 2, row // 2
    module = (iota((1, rows), 1) // tok) % 2 == 1
    share = jnp.where(module, loss_scale * mtp_share, loss_scale).astype(f32)
    peaks, masses, moments, picks = (ev_ref[:, k * rows : (k + 1) * rows] for k in range(4))
    sender = iota((ev_ref.shape[0], 1), 0) % 2

    def combine(which):
        mine = sender == which
        top = jnp.max(jnp.where(mine, peaks, -jnp.inf), axis=0, keepdims=True)
        drop = jnp.where(mine, peaks - top, 0.0)
        factor = jnp.where(mine, jnp.exp(drop), 0.0)
        total = jnp.sum(factor * masses, axis=0, keepdims=True)
        spread = jnp.sum(factor * (moments + drop * masses), axis=0, keepdims=True) / total
        picked = jnp.sum(jnp.where(mine, picks, 0.0), axis=0, keepdims=True)
        return top, total, share * (spread - (picked - top)) / width

    top, total, dot_own = combine(core)
    dot_other = combine(1 - core)[2]
    dot_ref[...] = in_order(jnp.concatenate([dot_own, dot_other], axis=1), tok, dot_ref.shape[0])
    hit = jnp.where(vocab_rows(vrows) == tgt_ref[...], 1.0, 0.0)
    gt = (share * (jnp.exp(lt_ref[...] - top) / total - hit)).astype(bf16)
    own_ref[...] = gt[:vrows]
    away_ref[...] = gt[vrows:]
    column, main = outs[:nvoc], outs[nvoc:]
    half = rows // 2
    line, col = iota((rows, rows), 0), iota((rows, rows), 1)
    spot = line % half
    want = jnp.where(
        line < half, spot // tok * 2 * tok + tok, (spot // tok ^ chip) * 2 * tok
    )
    pick = onehot(col == want + spot % tok)
    grads = matmul(pick, gt[:vrows], NT).astype(bf16)
    others = matmul(pick, gt[vrows:], NT).astype(bf16)
    cols = width // nvoc
    for k in range(nvoc):
        at = pl.ds(pl.multiple_of((voc ^ k) * cols, 128), cols)
        total = matmul(grads, w_ref[:, at]) + matmul(others, part_ref[:, at])
        column[k][...] = total[:half].astype(bf16)
        for j, out in enumerate(main):
            out[:, at] = total[half + j * tok : half + (j + 1) * tok].astype(bf16)


def rest_kernel(tok, raw_ref, gain_ref, hid_ref, own_ref, got_ref, hid_out, gt_out):
    f32, bf16 = jnp.float32, jnp.bfloat16
    rows, width = hid_ref.shape
    module = (iota((rows, 1), 0) // tok) % 2 == 1
    inverse = jnp.sum(raw_ref[:, width:].astype(f32), axis=1, keepdims=True)
    for c in chunks(width):
        x = raw_ref[:, c].astype(f32)
        hid_out[:rows, c] = hid_ref[:, c]
        hid_out[rows:, c] = jnp.where(module, x * inverse * gain_ref[:, c], x).astype(bf16)
    gt_out[:, :rows] = own_ref[...]
    gt_out[:, rows:] = got_ref[...]


def column_kernel(nvoc, attn_ref, *refs):
    f32, bf16 = jnp.float32, jnp.bfloat16
    parts, outs = refs[:nvoc], refs[nvoc:]
    _, cols = parts[0].shape
    chip = lax.axis_index("rows") // 2
    total = tree_sum([p[...].astype(f32) for p in parts]).astype(bf16)
    tok, heads, _ = attn_ref.shape
    each = heads // len(outs)
    line, spot = iota((each, heads), 0), iota((each, heads), 1)
    for j, out in enumerate(outs):
        out[:, :cols] = total
        pick = onehot(spot == (chip ^ j) * each + line)
        tail = jnp.concatenate([matmul(pick, attn_ref[i]) for i in range(tok)], axis=0)
        out[:, cols:] = tail.astype(bf16)


def main_kernel(*refs):
    for c in chunks(refs[-1].shape[1]):
        refs[-1][:, c] = tree_sum([m[:, c].astype(jnp.float32) for m in refs[:-1]]).astype(
            jnp.bfloat16
        )


def plane_kernel(tok, nchip, *refs):
    f32, bf16 = jnp.float32, jnp.bfloat16
    parts, (swap_ref, val_ref) = refs[:nchip], refs[nchip:]
    nmod, hdim = val_ref.shape
    size = parts[0].shape[1] - swap_ref.shape[1] + hdim
    cols = swap_ref.shape[1] - hdim
    each, heads = parts[0].shape[0] // tok, hdim // size
    swap_ref[:, :cols] = tree_sum([p[:, :cols].astype(f32) for p in parts]).astype(bf16)
    held = jnp.concatenate([p[:, cols:].astype(f32) for p in parts], axis=0).astype(bf16)
    core = lax.axis_index("rows") % 2
    line, spot = iota((nmod, held.shape[0]), 0), iota((nmod, held.shape[0]), 1)
    for h in range(heads):
        at = line * each + h
        lanes = slice(h * size, (h + 1) * size)
        val_ref[:, lanes] = matmul(onehot(spot == at + core * heads), held).astype(bf16)
        away = matmul(onehot(spot == at + (1 - core) * heads), held)
        swap_ref[:, cols + h * size : cols + (h + 1) * size] = away.astype(bf16)


def last_kernel(
    tok, raw_ref, part_ref, inv_ref, dot_ref, gain_ref, proj_ref, own_ref, other_ref, val_ref, res_ref, val_out, *outs
):
    f32, bf16 = jnp.float32, jnp.bfloat16
    parcels, (scratch,) = outs[:-1], outs[-1:]
    half = raw_ref.shape[0]
    rows = 2 * half
    hdim, cols = proj_ref.shape
    nmod = own_ref.shape[0]
    nvoc = len(parcels)
    row, voc = lax.axis_index("rows"), lax.axis_index("vocab")
    core, chip = row % 2, row // 2
    line, spot = iota((half, nmod), 0), iota((half, nmod), 1)
    owner = line // tok
    same = spot == (owner // 2) * tok + line % tok
    grad = matmul(onehot(same & (owner % 2 == core)), own_ref[:, :cols])
    grad += matmul(onehot(same & (owner % 2 != core)), other_ref[:, :cols])
    start = pl.multiple_of(voc * cols, 128)
    far = jnp.sum(part_ref[:, gain_ref.shape[1] :].astype(f32), axis=1, keepdims=True)
    near = jnp.concatenate([across(inv_ref[...]), across(far)], axis=1)
    inverse = in_order(near, tok, half)
    at = pl.ds(start, cols)
    state = jnp.concatenate([raw_ref[:, at], part_ref[:, at]], axis=0)
    normed = matmul(onehot(module_lines(half, rows, tok)), state) * inverse
    gain_piece = jnp.sum(grad * normed, axis=0, keepdims=True)
    gain = gain_ref[:, pl.ds(start, cols)]
    scaled = grad * gain
    residual = (inverse * (scaled - normed * dot_ref[...])).astype(bf16)
    res_ref[...] = residual
    scratch[...] = matmul(residual, proj_ref[...], NT)
    tok_voc = half // nvoc
    fold = tok_voc // tok
    strip = cols // fold
    line, spot = iota((tok_voc, half), 0), iota((tok_voc, half), 1)
    mine = sum(
        matmul(
            onehot((line // tok == f) & (spot == row * tok + line % tok)),
            residual[:, f * strip : (f + 1) * strip],
        )
        for f in range(fold)
    ).astype(bf16)
    pieces = [gain_piece[:, c : c + hdim] for c in range(0, cols, hdim)]
    pieces += [jnp.zeros((1, hdim), f32)] * (tok_voc - len(pieces))
    gains = jnp.concatenate(pieces, axis=0)
    gains = gains.astype(bf16)
    for k, out in enumerate(parcels):
        block = scratch[pl.ds(pl.multiple_of((voc ^ k) * tok_voc, tok_voc), tok_voc), :]
        out[:, :strip] = mine
        out[:, strip : strip + hdim] = block.astype(bf16)
        out[:, strip + hdim :] = gains
    line, spot = iota((half, nmod), 0), iota((half, nmod), 1)
    owner = line // tok
    same = spot == ((owner // 2) ^ chip) * tok + line % tok
    values = matmul(onehot(same & (owner % 2 == core)), val_ref[...])
    values += matmul(onehot(same & (owner % 2 != core)), other_ref[:, cols:])
    val_out[...] = values.astype(bf16)


def proj_kernel(val_ref, res_ref, out_ref):
    out_ref[...] = matmul(val_ref[...], res_ref[...], (((0,), (0,)), ((), ()))).astype(out_ref.dtype)


def output_kernel(tok, nvoc, cols, hold_ref, *refs):
    f32, bf16 = jnp.float32, jnp.bfloat16
    parts, mains = refs[:nvoc], refs[nvoc : nvoc + 2]
    trunk_ref, res_ref, gain_ref, attn_ref = refs[nvoc + 2 :]
    count, heads, size = attn_ref.shape
    hdim = heads * size
    fold = count // tok
    strip = cols // fold
    voc = lax.axis_index("vocab")
    values = [p[...].astype(f32) for p in parts]
    for k, part in enumerate(values):
        for f in range(fold):
            at = pl.ds(pl.multiple_of((voc ^ k) * cols + f * strip, 128), strip)
            res_ref[:, at] = part[f * tok : (f + 1) * tok, :strip].astype(bf16)
        gains = part[:, strip + hdim :]
        for i in range(cols // hdim):
            at = pl.ds(pl.multiple_of((voc ^ k) * cols + i * hdim, 128), hdim)
            gain_ref[:, at] = gains[i : i + 1]
    total = tree_sum([v[:, strip : strip + hdim] for v in values])
    for i in range(count):
        attn_ref[i] = jnp.concatenate(
            [total[i : i + 1, h * size : (h + 1) * size] for h in range(heads)], axis=0
        ).astype(bf16)
    for c in chunks(trunk_ref.shape[1]):
        trunk_ref[:, c] = tree_sum([m[:, c].astype(f32) for m in mains]).astype(bf16)


def local(
    trunk_hidden,
    mtp_state,
    mtp_gain,
    head_weight,
    target_ids,
    mtp_target_ids,
    attn_values,
    out_proj,
):
    f32, bf16 = jnp.float32, jnp.bfloat16
    tok, width = trunk_hidden.shape
    nrow = lax.axis_size("rows")
    nvoc = lax.axis_size("vocab")
    nchip = nrow // 2
    vrows = head_weight.shape[0]
    hdim, cols = out_proj.shape
    _, size = attn_values.shape[1:]
    ntok = nrow * tok
    nmod = nchip * tok
    tok_voc = ntok // nvoc
    part = functools.partial

    stacked = jnp.concatenate([trunk_hidden, mtp_state], axis=0)
    blocks = swaps([stacked] * nchip, "rows", 2)
    weight_near = swap(head_weight, "rows", 1)
    weight, gain, targets = kernel_call(
        part(prepare_kernel, tok),
        [((vrows, width), bf16), ((1, width), f32), ((1, ntok), jnp.int32)],
        head_weight,
        mtp_gain.reshape(width // 128, 128),
        target_ids.reshape(1, ntok),
        mtp_target_ids.reshape(1, ntok),
    )
    raw, hidden, logits, inverse, stats = kernel_call(
        part(head_kernel, tok, nchip),
        [
            ((ntok, width + 128), bf16),
            ((ntok, width), bf16),
            ((2 * vrows, ntok), f32),
            ((ntok, 1), f32),
            ((nrow * nvoc, 4 * ntok), f32),
        ],
        *blocks,
        weight,
        weight_near,
        gain,
        targets,
    )
    raw_near = swap(raw, "rows", 1)
    everyone = lax.all_to_all(
        stats, ("vocab", "rows"), split_axis=0, concat_axis=0, tiled=True
    )
    grads, grads_away, dot_mean, *pieces = kernel_call(
        part(loss_kernel, tok, nvoc),
        [((vrows, ntok), bf16)] * 2
        + [((ntok, 1), f32)]
        + [((nmod, cols), bf16)] * nvoc
        + [((tok, width), bf16)] * nchip,
        everyone,
        logits,
        targets,
        weight,
        weight_near,
    )
    column, main = pieces[:nvoc], pieces[nvoc:]
    column = swaps(column, "vocab", 1)
    main = swaps(main, "rows", 2)
    grads_near = swap(grads_away, "rows", 1)
    hidden, logit_grads = kernel_call(
        part(rest_kernel, tok),
        [((2 * ntok, width), bf16), ((vrows, 2 * ntok), bf16)],
        raw_near,
        gain,
        hidden,
        grads,
        grads_near,
    )
    grad_head = lax.dot_general(
        logit_grads, hidden, (((1,), (0,)), ((), ())), preferred_element_type=f32
    ).astype(bf16)
    plane = kernel_call(
        part(column_kernel, nvoc),
        [((nmod, cols + size), bf16)] * nchip,
        attn_values,
        *column,
    )
    plane = swaps(plane, "rows", 2)
    (main,) = kernel_call(main_kernel, [((tok, width), bf16)], *main)
    near = swap(main, "vocab", 1)
    module, own_values = kernel_call(
        part(plane_kernel, tok, nchip),
        [((nmod, cols + hdim), bf16), ((nmod, hdim), bf16)],
        *plane,
    )
    (main,) = kernel_call(main_kernel, [((tok, width), bf16)], main, near)
    main = [main, swap(main, "vocab", 2)]
    other = swap(module, "rows", 1)
    residual, values, *parcels = kernel_call(
        part(last_kernel, tok),
        [((ntok, cols), bf16), ((ntok, hdim), bf16)]
        + [((tok_voc, cols * tok // tok_voc + 2 * hdim), bf16)] * nvoc,
        raw,
        raw_near,
        inverse,
        dot_mean,
        gain,
        out_proj,
        module,
        other,
        own_values,
        side=[pltpu.VMEM((ntok, hdim), f32)],
    )
    parcels = swaps(parcels, "vocab", 1)
    (grad_out_proj,) = kernel_call(proj_kernel, [((hdim, cols), bf16)], values, residual)
    grad_trunk, grad_residual, grad_gain, grad_attn = kernel_call(
        part(output_kernel, tok, nvoc, cols),
        [
            ((tok, width), bf16),
            ((tok, width), bf16),
            ((1, width), f32),
            ((tok_voc, hdim // size, size), bf16),
        ],
        grad_head,
        *parcels,
        *main,
        away=(0,),
    )
    return (
        grad_trunk,
        grad_residual,
        grad_gain.reshape(width),
        grad_head,
        grad_attn,
        grad_out_proj,
    )


def swaps(parts, axis, unit):
    got = [parts[0]]
    for k in range(1, len(parts)):
        got.append(swap(parts[k], axis, k * unit))
    return got


def choose(*args):
    tok, cols, hdim = args[0].shape[0], args[7].shape[1], args[7].shape[0]
    ntok = lax.axis_size("rows") * tok
    tok_voc = ntok // lax.axis_size("vocab")
    fits = (
        lax.axis_size("rows") == 8
        and ntok == 32
        and         tok_voc == 8
        and lax.axis_size("vocab") == 4
        and tok_voc % tok == 0
        and cols % (128 * tok_voc // tok) == 0
        and hdim % 128 == 0
        and cols % hdim == 0
        and cols // hdim <= tok_voc
        and args[6].shape[1] // (lax.axis_size("rows") // 2) == tok
    )
    if not fits:
        return plain(*args)
    return local(*args)


def solution(mesh):
    return jax.shard_map(
        choose,
        mesh=mesh,
        in_specs=(
            P("rows", None),
            P("rows", None),
            P(),
            P(("vocab", "rows"), None),
            P(),
            P(),
            P("rows", None, None),
            P("rows", "vocab"),
        ),
        out_specs=(
            P("rows", None),
            P("rows", None),
            P(),
            P(("vocab", "rows"), None),
            P("vocab", "rows", None),
            P("rows", "vocab"),
        ),
        check_vma=False,
    )
```

```python
import functools

import jax
import jax.numpy as jnp
from jax import lax
from jax.experimental import pallas as pl
from jax.experimental.pallas import tpu as pltpu
from jax.sharding import PartitionSpec as P

loss_scale = 8.0
mtp_share = 0.3
norm_eps = 1e-06


def swap(x, axis, k):
    n = lax.axis_size(axis)
    return lax.ppermute(x, axis, [(i, i ^ k) for i in range(n)])


def tree_sum(parts):
    while len(parts) > 1:
        parts = [a + b for a, b in zip(parts[::2], parts[1::2])]
    return parts[0]


def plain(
    trunk_hidden,
    mtp_state,
    mtp_gain,
    head_weight,
    target_ids,
    mtp_target_ids,
    attn_values,
    out_proj,
):
    f32, bf16 = jnp.float32, jnp.bfloat16
    tok, width = trunk_hidden.shape
    nrow = lax.axis_size("rows")
    nvoc = lax.axis_size("vocab")
    ndev = nrow * nvoc
    nchip = nrow // 2
    row = lax.axis_index("rows")
    voc = lax.axis_index("vocab")
    core = row & 1
    chip = row >> 1
    vrows = head_weight.shape[0]
    cols = out_proj.shape[1]
    hdim = out_proj.shape[0]
    ntok = nrow * tok
    gain = mtp_gain.astype(f32)

    stacked = jnp.concatenate([trunk_hidden, mtp_state], axis=0)
    gathered = lax.all_gather(stacked, "rows", axis=0, tiled=True).reshape(nrow, 2, tok, width)
    state = gathered[:, 1].astype(f32)
    inverse = lax.rsqrt(jnp.mean(state * state, axis=-1, keepdims=True) + norm_eps)
    mtp_hidden = (state * inverse * gain).astype(bf16)
    hidden = jnp.stack([gathered[:, 0], mtp_hidden], axis=1).reshape(2 * ntok, width)

    targets = jnp.stack(
        [target_ids.reshape(nrow, tok), mtp_target_ids.reshape(nrow, tok)], axis=1
    ).reshape(-1)
    shares = jnp.broadcast_to(
        jnp.array([loss_scale, loss_scale * mtp_share], f32)[None, :, None], (nrow, 2, tok)
    ).reshape(-1)
    vocab_ids = (voc * nrow + row) * vrows + jnp.arange(vrows, dtype=jnp.int32)
    onehot = targets[:, None] == vocab_ids[None, :]

    logits = lax.dot_general(
        hidden, head_weight, (((1,), (1,)), ((), ())), preferred_element_type=f32
    )
    peak = jnp.max(logits, axis=1)
    below = logits - peak[:, None]
    weight = jnp.exp(below)
    mass = jnp.sum(weight, axis=1)
    moment = jnp.sum(weight * below, axis=1)
    picked = jnp.sum(jnp.where(onehot, logits, 0.0), axis=1)
    stats = jnp.stack([peak, mass, moment, picked])
    everyone = lax.all_to_all(
        jnp.broadcast_to(stats[None], (ndev,) + stats.shape),
        ("vocab", "rows"),
        split_axis=0,
        concat_axis=0,
        tiled=True,
    )
    peaks, masses, moments, picks = (everyone[:, k] for k in range(4))
    top = jnp.max(peaks, axis=0)
    drop = peaks - top
    factor = jnp.exp(drop)
    total = jnp.sum(factor * masses, axis=0)
    spread = jnp.sum(factor * (moments + drop * masses), axis=0) / total
    dot_mean = shares * (spread - (jnp.sum(picks, axis=0) - top)) / width
    dot_mean = dot_mean.reshape(nrow, 2, tok)[:, 1].reshape(ntok, 1)

    logit_grads = (
        shares[:, None] * (jnp.exp(logits - top[:, None]) / total[:, None] - onehot.astype(f32))
    ).astype(bf16)

    by_core = logit_grads.reshape(nchip, 2, 2, tok, vrows)

    def rows_for(which):
        part = lax.dynamic_index_in_dim(by_core, which, 1, keepdims=False)
        own = [lax.dynamic_index_in_dim(part, chip ^ j, 0, keepdims=False)[0] for j in range(nchip)]
        return jnp.concatenate([part[:, 1].reshape(nchip * tok, vrows)] + own, axis=0)

    def grads_of(rows):
        return jnp.dot(rows, head_weight, preferred_element_type=f32).astype(bf16)

    away = grads_of(rows_for(1 - core))
    kept = grads_of(rows_for(core))
    pair = (kept.astype(f32) + swap(away, "rows", 1).astype(f32)).astype(bf16)

    def columns_for(k):
        return lax.dynamic_slice_in_dim(pair, (voc ^ k) * cols, cols, 1)

    column_sum = tree_sum(
        [columns_for(0).astype(f32)]
        + [swap(columns_for(k), "vocab", k).astype(f32) for k in range(1, nvoc)]
    ).astype(bf16)
    nmod = nchip * tok
    module, main = column_sum[:nmod], column_sum[nmod:].reshape(nchip, tok, cols)
    plane = [jnp.concatenate([module, main[0]], axis=0)] + [
        swap(jnp.concatenate([module, main[j]], axis=0), "rows", 2 * j) for j in range(1, nchip)
    ]
    plane_sum = tree_sum([part.astype(f32) for part in plane]).astype(bf16)
    module, trunk_piece = plane_sum[:nmod], plane_sum[nmod:]
    other = swap(module, "rows", 1)

    grad_head = lax.dot_general(
        logit_grads, hidden, (((0,), (0,)), ((), ())), preferred_element_type=f32
    ).astype(bf16)
    values = lax.all_to_all(attn_values, "rows", split_axis=1, concat_axis=0, tiled=True)
    values = values.reshape(ntok, hdim)

    first = jnp.where(core == 0, module, other).reshape(nchip, 1, tok, cols)
    second = jnp.where(core == 0, other, module).reshape(nchip, 1, tok, cols)
    mtp_grad = jnp.concatenate([first, second], axis=1).reshape(ntok, cols).astype(f32)
    inv = inverse.reshape(ntok, 1)
    normed = lax.dynamic_slice_in_dim(
        gathered[:, 1].reshape(ntok, width), voc * cols, cols, 1
    ).astype(f32) * inv
    gain_piece = jnp.sum(mtp_grad * normed, axis=0, keepdims=True)
    scaled = mtp_grad * lax.dynamic_slice_in_dim(gain, voc * cols, cols, 0)
    residual = (inv * (scaled - normed * dot_mean)).astype(bf16)
    attn_terms = lax.dot_general(
        residual, out_proj, (((1,), (1,)), ((), ())), preferred_element_type=f32
    ).astype(bf16)
    grad_out_proj = lax.dot_general(
        values, residual, (((0,), (0,)), ((), ())), preferred_element_type=f32
    ).astype(bf16)

    residual_piece = lax.dynamic_slice_in_dim(residual, row * tok, tok, 0)
    gain_high = gain_piece.astype(bf16)
    gain_low = (gain_piece - gain_high.astype(f32)).astype(bf16)
    tok_voc = ntok // nvoc
    lines = -(-tok_voc * hdim // cols)
    terms = attn_terms.reshape(nvoc, tok_voc * hdim)
    terms = jnp.pad(terms, ((0, 0), (0, lines * cols - tok_voc * hdim))).reshape(nvoc, lines, cols)
    shared = jnp.concatenate([trunk_piece, residual_piece, gain_high, gain_low], axis=0)

    def parcel(k):
        mine = lax.dynamic_index_in_dim(terms, voc ^ k, 0, keepdims=False)
        return jnp.concatenate([shared, mine], axis=0)

    parcels = [parcel(0)] + [swap(parcel(k), "vocab", k) for k in range(1, nvoc)]
    ordered = jnp.stack(parcels)
    grad_attn = jnp.sum(ordered[:, 2 * tok + 2 :].astype(f32), axis=0).astype(bf16)
    grad_attn = grad_attn.reshape(-1)[: tok_voc * hdim].reshape(
        tok_voc, hdim // attn_values.shape[2], attn_values.shape[2]
    )
    pieces = [
        lax.dynamic_index_in_dim(ordered, voc ^ k, 0, keepdims=False)[: 2 * tok + 2]
        for k in range(nvoc)
    ]
    whole = jnp.concatenate(pieces, axis=1)
    grad_trunk = whole[:tok]
    grad_residual = whole[tok : 2 * tok]
    grad_gain = whole[2 * tok].astype(f32) + whole[2 * tok + 1].astype(f32)
    return (grad_trunk, grad_residual, grad_gain, grad_head, grad_attn, grad_out_proj)


NT = (((1,), (1,)), ((), ()))
NN = (((1,), (0,)), ((), ()))


def iota(shape, dim):
    return lax.broadcasted_iota(jnp.int32, shape, dim)


def matmul(a, b, dims=NN):
    return lax.dot_general(a, b, dims, preferred_element_type=jnp.float32)


def onehot(mask):
    return jnp.where(mask, 1.0, 0.0).astype(jnp.bfloat16)


def chunks(width):
    step = next(s for s in (1024, 512, 256, 128) if width % s == 0)
    return [slice(c, c + step) for c in range(0, width, step)]


def kernel_call(body, outs, *args, side=None, away=()):
    vmem, hbm = pl.BlockSpec(memory_space=pltpu.VMEM), pl.BlockSpec(memory_space=pltpu.HBM)
    return pl.pallas_call(
        body,
        in_specs=[hbm if k in away else vmem for k in range(len(args))],
        out_specs=[vmem] * len(outs),
        out_shape=[jax.ShapeDtypeStruct(s, d) for s, d in outs],
        scratch_shapes=side or [],
        compiler_params=pltpu.CompilerParams(vmem_limit_bytes=16 << 20),
    )(*args)


def module_lines(half, rows, tok):
    line, spot = iota((half, rows), 0), iota((half, rows), 1)
    owner = line // tok
    block = (owner % 2 ^ lax.axis_index("rows") % 2) * (half // tok // 2) + owner // 2
    return spot == block * 2 * tok + tok + line % tok


def in_order(near, tok, half):
    pick = module_lines(half, near.shape[1], tok)
    return jnp.sum(jnp.where(pick, near, 0.0), axis=1, keepdims=True)


def across(column):
    eye = iota((column.shape[0],) * 2, 0) == iota((column.shape[0],) * 2, 1)
    return jnp.sum(jnp.where(eye, column, 0.0), axis=0, keepdims=True)


def vocab_rows(vrows):
    row = lax.axis_index("rows")
    base = lax.axis_index("vocab") * lax.axis_size("rows")
    line = iota((2 * vrows, 1), 0)
    own = line < vrows
    return jnp.where(own, (base + row) * vrows + line, (base + (row ^ 1)) * vrows + line - vrows)


def prepare_kernel(tok, w_src, gain_src, ids_ref, mids_ref, w_ref, gain_ref, tgt_ref):
    f32 = jnp.float32
    w_ref[...] = w_src[...]
    gains = gain_src[...].astype(f32)
    for k in range(gains.shape[0]):
        gain_ref[:, k * 128 : (k + 1) * 128] = gains[k : k + 1]
    half, rows = ids_ref.shape[1], tgt_ref.shape[1]
    eye = iota((half, half), 0) == iota((half, half), 1)
    main = jnp.sum(jnp.where(eye, ids_ref[...], 0), axis=1, keepdims=True)
    other = jnp.sum(jnp.where(eye, mids_ref[...], 0), axis=1, keepdims=True)
    src, dst = iota((half, rows), 0), iota((half, rows), 1)
    own = src // tok % 2 == lax.axis_index("rows") % 2
    place = src // tok // 2 * 2 * tok + src % tok
    tgt = jnp.where(own & (dst == place), main, 0) + jnp.where(own & (dst == place + tok), other, 0)
    tgt_ref[...] = jnp.sum(tgt, axis=0, keepdims=True)


def inverse_of(x_ref, at):
    width = x_ref.shape[1]
    square = sum(jnp.square(x_ref[at, c].astype(jnp.float32)) for c in chunks(width))
    return lax.rsqrt(jnp.sum(square, axis=1, keepdims=True) / width + norm_eps)


def head_kernel(tok, count, *refs):
    f32, bf16 = jnp.float32, jnp.bfloat16
    blocks, (w_ref, part_ref, gain_ref, tgt_ref) = refs[:count], refs[count : count + 4]
    raw_ref, hid_ref, lt_ref, inv_ref, msg_ref = refs[count + 4 :]
    size, width = blocks[0].shape
    rows, vrows = count * size, w_ref.shape[0]
    chip = lax.axis_index("rows") // 2
    module = iota((size, 1), 0) // tok % 2 == 1
    inverses = [inverse_of(block, slice(None)) for block in blocks]
    places = [pl.ds(pl.multiple_of((chip ^ k) * size, size), size) for k in range(count)]
    for k in range(count):
        inv_ref[places[k]] = inverses[k]
    own = jnp.zeros((vrows, rows), f32)
    other = jnp.zeros((vrows, rows), f32)
    for c in chunks(width):
        gain = gain_ref[:, c]
        for k, block in enumerate(blocks):
            raw = block[:, c]
            x = raw.astype(f32)
            raw_ref[places[k], c] = raw
            hid_ref[places[k], c] = jnp.where(module, x * inverses[k] * gain, x).astype(bf16)
        h = hid_ref[:, c]
        own += matmul(w_ref[:, c], h, NT)
        other += matmul(part_ref[:, c], h, NT)
    lt = jnp.concatenate([own, other], axis=0)
    lt_ref[...] = lt
    left, tail = inv_ref[...], jnp.zeros((rows, 128), f32)
    for k in range(3):
        term = left.astype(bf16).astype(f32)
        tail = jnp.where(iota(tail.shape, 1) == k, term, tail)
        left = left - term
    raw_ref[:, width:] = tail.astype(bf16)
    peak = jnp.max(lt, axis=0, keepdims=True)
    below = lt - peak
    weight = jnp.exp(below)
    picked = jnp.where(vocab_rows(vrows) == tgt_ref[...], lt, 0.0)
    for k, stat in enumerate(
        (
            peak,
            jnp.sum(weight, axis=0, keepdims=True),
            jnp.sum(weight * below, axis=0, keepdims=True),
            jnp.sum(picked, axis=0, keepdims=True),
        )
    ):
        msg_ref[:, k * rows : (k + 1) * rows] = jnp.broadcast_to(stat, (msg_ref.shape[0], rows))


def loss_kernel(tok, nvoc, ev_ref, lt_ref, tgt_ref, w_ref, part_ref, own_ref, away_ref, dot_ref, *outs):
    f32, bf16 = jnp.float32, jnp.bfloat16
    vrows, width = w_ref.shape
    rows = lt_ref.shape[1]
    row, voc = lax.axis_index("rows"), lax.axis_index("vocab")
    core, chip = row % 2, row // 2
    module = (iota((1, rows), 1) // tok) % 2 == 1
    share = jnp.where(module, loss_scale * mtp_share, loss_scale).astype(f32)
    peaks, masses, moments, picks = (ev_ref[:, k * rows : (k + 1) * rows] for k in range(4))
    sender = iota((ev_ref.shape[0], 1), 0) // nvoc % 2

    def combine(which):
        mine = sender == which
        top = jnp.max(jnp.where(mine, peaks, -jnp.inf), axis=0, keepdims=True)
        drop = jnp.where(mine, peaks - top, 0.0)
        factor = jnp.where(mine, jnp.exp(drop), 0.0)
        total = jnp.sum(factor * masses, axis=0, keepdims=True)
        spread = jnp.sum(factor * (moments + drop * masses), axis=0, keepdims=True) / total
        picked = jnp.sum(jnp.where(mine, picks, 0.0), axis=0, keepdims=True)
        return top, total, share * (spread - (picked - top)) / width

    top, total, dot_own = combine(core)
    dot_other = combine(1 - core)[2]
    dot_ref[...] = in_order(jnp.concatenate([dot_own, dot_other], axis=1), tok, dot_ref.shape[0])
    hit = jnp.where(vocab_rows(vrows) == tgt_ref[...], 1.0, 0.0)
    gt = (share * (jnp.exp(lt_ref[...] - top) / total - hit)).astype(bf16)
    own_ref[...] = gt[:vrows]
    away_ref[...] = gt[vrows:]
    column, main = outs[:nvoc], outs[nvoc:]
    half = rows // 2
    line, col = iota((rows, rows), 0), iota((rows, rows), 1)
    spot = line % half
    want = jnp.where(
        line < half, spot // tok * 2 * tok + tok, (spot // tok ^ chip) * 2 * tok
    )
    pick = onehot(col == want + spot % tok)
    grads = matmul(pick, gt[:vrows], NT).astype(bf16)
    others = matmul(pick, gt[vrows:], NT).astype(bf16)
    cols = width // nvoc
    for k in range(nvoc):
        at = pl.ds(pl.multiple_of((voc ^ k) * cols, 128), cols)
        total = matmul(grads, w_ref[:, at]) + matmul(others, part_ref[:, at])
        column[k][...] = total[:half].astype(bf16)
        for j, out in enumerate(main):
            out[:, at] = total[half + j * tok : half + (j + 1) * tok].astype(bf16)


def rest_kernel(tok, raw_ref, gain_ref, hid_ref, own_ref, got_ref, hid_out, gt_out):
    f32, bf16 = jnp.float32, jnp.bfloat16
    rows, width = hid_ref.shape
    module = (iota((rows, 1), 0) // tok) % 2 == 1
    inverse = jnp.sum(raw_ref[:, width:].astype(f32), axis=1, keepdims=True)
    for c in chunks(width):
        x = raw_ref[:, c].astype(f32)
        hid_out[:rows, c] = hid_ref[:, c]
        hid_out[rows:, c] = jnp.where(module, x * inverse * gain_ref[:, c], x).astype(bf16)
    gt_out[:, :rows] = own_ref[...]
    gt_out[:, rows:] = got_ref[...]


def column_kernel(nvoc, attn_ref, *refs):
    f32, bf16 = jnp.float32, jnp.bfloat16
    parts, outs = refs[:nvoc], refs[nvoc:]
    _, cols = parts[0].shape
    chip = lax.axis_index("rows") // 2
    total = tree_sum([p[...].astype(f32) for p in parts]).astype(bf16)
    tok, heads, _ = attn_ref.shape
    each = heads // len(outs)
    line, spot = iota((each, heads), 0), iota((each, heads), 1)
    for j, out in enumerate(outs):
        out[:, :cols] = total
        pick = onehot(spot == (chip ^ j) * each + line)
        tail = jnp.concatenate([matmul(pick, attn_ref[i]) for i in range(tok)], axis=0)
        out[:, cols:] = tail.astype(bf16)


def main_kernel(*refs):
    for c in chunks(refs[-1].shape[1]):
        refs[-1][:, c] = tree_sum([m[:, c].astype(jnp.float32) for m in refs[:-1]]).astype(
            jnp.bfloat16
        )


def plane_kernel(tok, nchip, *refs):
    f32, bf16 = jnp.float32, jnp.bfloat16
    parts, (swap_ref, val_ref) = refs[:nchip], refs[nchip:]
    nmod, hdim = val_ref.shape
    size = parts[0].shape[1] - swap_ref.shape[1] + hdim
    cols = swap_ref.shape[1] - hdim
    each, heads = parts[0].shape[0] // tok, hdim // size
    swap_ref[:, :cols] = tree_sum([p[:, :cols].astype(f32) for p in parts]).astype(bf16)
    held = jnp.concatenate([p[:, cols:].astype(f32) for p in parts], axis=0).astype(bf16)
    core = lax.axis_index("rows") % 2
    line, spot = iota((nmod, held.shape[0]), 0), iota((nmod, held.shape[0]), 1)
    for h in range(heads):
        at = line * each + h
        lanes = slice(h * size, (h + 1) * size)
        val_ref[:, lanes] = matmul(onehot(spot == at + core * heads), held).astype(bf16)
        away = matmul(onehot(spot == at + (1 - core) * heads), held)
        swap_ref[:, cols + h * size : cols + (h + 1) * size] = away.astype(bf16)


def last_kernel(
    tok, raw_ref, part_ref, inv_ref, dot_ref, gain_ref, proj_ref, own_ref, other_ref, val_ref, res_ref, val_out, *outs
):
    f32, bf16 = jnp.float32, jnp.bfloat16
    parcels, (scratch,) = outs[:-1], outs[-1:]
    half = raw_ref.shape[0]
    rows = 2 * half
    hdim, cols = proj_ref.shape
    nmod = own_ref.shape[0]
    nvoc = len(parcels)
    row, voc = lax.axis_index("rows"), lax.axis_index("vocab")
    core, chip = row % 2, row // 2
    line, spot = iota((half, nmod), 0), iota((half, nmod), 1)
    owner = line // tok
    same = spot == (owner // 2) * tok + line % tok
    grad = matmul(onehot(same & (owner % 2 == core)), own_ref[:, :cols])
    grad += matmul(onehot(same & (owner % 2 != core)), other_ref[:, :cols])
    start = pl.multiple_of(voc * cols, 128)
    far = jnp.sum(part_ref[:, gain_ref.shape[1] :].astype(f32), axis=1, keepdims=True)
    near = jnp.concatenate([across(inv_ref[...]), across(far)], axis=1)
    inverse = in_order(near, tok, half)
    at = pl.ds(start, cols)
    state = jnp.concatenate([raw_ref[:, at], part_ref[:, at]], axis=0)
    normed = matmul(onehot(module_lines(half, rows, tok)), state) * inverse
    gain_piece = jnp.sum(grad * normed, axis=0, keepdims=True)
    gain = gain_ref[:, pl.ds(start, cols)]
    scaled = grad * gain
    residual = (inverse * (scaled - normed * dot_ref[...])).astype(bf16)
    res_ref[...] = residual
    scratch[...] = matmul(residual, proj_ref[...], NT)
    tok_voc = half // nvoc
    fold = tok_voc // tok
    strip = cols // fold
    line, spot = iota((tok_voc, half), 0), iota((tok_voc, half), 1)
    mine = sum(
        matmul(
            onehot((line // tok == f) & (spot == row * tok + line % tok)),
            residual[:, f * strip : (f + 1) * strip],
        )
        for f in range(fold)
    ).astype(bf16)
    pieces = [gain_piece[:, c : c + hdim] for c in range(0, cols, hdim)]
    pieces += [jnp.zeros((1, hdim), f32)] * (tok_voc - len(pieces))
    gains = jnp.concatenate(pieces, axis=0)
    high = gains.astype(bf16)
    low = (gains - high.astype(f32)).astype(bf16)
    for k, out in enumerate(parcels):
        block = scratch[pl.ds(pl.multiple_of((voc ^ k) * tok_voc, tok_voc), tok_voc), :]
        out[:, :strip] = mine
        out[:, strip : strip + hdim] = block.astype(bf16)
        out[:, strip + hdim : strip + 2 * hdim] = high
        out[:, strip + 2 * hdim :] = low
    line, spot = iota((half, nmod), 0), iota((half, nmod), 1)
    owner = line // tok
    same = spot == ((owner // 2) ^ chip) * tok + line % tok
    values = matmul(onehot(same & (owner % 2 == core)), val_ref[...])
    values += matmul(onehot(same & (owner % 2 != core)), other_ref[:, cols:])
    val_out[...] = values.astype(bf16)


def proj_kernel(val_ref, res_ref, out_ref):
    out_ref[...] = matmul(val_ref[...], res_ref[...], (((0,), (0,)), ((), ()))).astype(out_ref.dtype)


def output_kernel(tok, nvoc, cols, hold_ref, *refs):
    f32, bf16 = jnp.float32, jnp.bfloat16
    parts, mains = refs[:nvoc], refs[nvoc : nvoc + 2]
    trunk_ref, res_ref, gain_ref, attn_ref = refs[nvoc + 2 :]
    count, heads, size = attn_ref.shape
    hdim = heads * size
    fold = count // tok
    strip = cols // fold
    voc = lax.axis_index("vocab")
    values = [p[...].astype(f32) for p in parts]
    for k, part in enumerate(values):
        for f in range(fold):
            at = pl.ds(pl.multiple_of((voc ^ k) * cols + f * strip, 128), strip)
            res_ref[:, at] = part[f * tok : (f + 1) * tok, :strip].astype(bf16)
        gains = part[:, strip + hdim : strip + 2 * hdim] + part[:, strip + 2 * hdim :]
        for i in range(cols // hdim):
            at = pl.ds(pl.multiple_of((voc ^ k) * cols + i * hdim, 128), hdim)
            gain_ref[:, at] = gains[i : i + 1]
    total = tree_sum([v[:, strip : strip + hdim] for v in values])
    for i in range(count):
        attn_ref[i] = jnp.concatenate(
            [total[i : i + 1, h * size : (h + 1) * size] for h in range(heads)], axis=0
        ).astype(bf16)
    for c in chunks(trunk_ref.shape[1]):
        trunk_ref[:, c] = tree_sum([m[:, c].astype(f32) for m in mains]).astype(bf16)


def local(
    trunk_hidden,
    mtp_state,
    mtp_gain,
    head_weight,
    target_ids,
    mtp_target_ids,
    attn_values,
    out_proj,
):
    f32, bf16 = jnp.float32, jnp.bfloat16
    tok, width = trunk_hidden.shape
    nrow = lax.axis_size("rows")
    nvoc = lax.axis_size("vocab")
    nchip = nrow // 2
    vrows = head_weight.shape[0]
    hdim, cols = out_proj.shape
    _, size = attn_values.shape[1:]
    ntok = nrow * tok
    nmod = nchip * tok
    tok_voc = ntok // nvoc
    part = functools.partial

    stacked = jnp.concatenate([trunk_hidden, mtp_state], axis=0)
    blocks = swaps([stacked] * nchip, "rows", 2)
    weight_near = swap(head_weight, "rows", 1)
    weight, gain, targets = kernel_call(
        part(prepare_kernel, tok),
        [((vrows, width), bf16), ((1, width), f32), ((1, ntok), jnp.int32)],
        head_weight,
        mtp_gain.reshape(width // 128, 128),
        target_ids.reshape(1, ntok),
        mtp_target_ids.reshape(1, ntok),
    )
    raw, hidden, logits, inverse, stats = kernel_call(
        part(head_kernel, tok, nchip),
        [
            ((ntok, width + 128), bf16),
            ((ntok, width), bf16),
            ((2 * vrows, ntok), f32),
            ((ntok, 1), f32),
            ((nrow * nvoc, 4 * ntok), f32),
        ],
        *blocks,
        weight,
        weight_near,
        gain,
        targets,
    )
    raw_near = swap(raw, "rows", 1)
    everyone = lax.all_to_all(
        stats, ("rows", "vocab"), split_axis=0, concat_axis=0, tiled=True
    )
    grads, grads_away, dot_mean, *pieces = kernel_call(
        part(loss_kernel, tok, nvoc),
        [((vrows, ntok), bf16)] * 2
        + [((ntok, 1), f32)]
        + [((nmod, cols), bf16)] * nvoc
        + [((tok, width), bf16)] * nchip,
        everyone,
        logits,
        targets,
        weight,
        weight_near,
    )
    column, main = pieces[:nvoc], pieces[nvoc:]
    column = swaps(column, "vocab", 1)
    main = swaps(main, "rows", 2)
    grads_near = swap(grads_away, "rows", 1)
    hidden, logit_grads = kernel_call(
        part(rest_kernel, tok),
        [((2 * ntok, width), bf16), ((vrows, 2 * ntok), bf16)],
        raw_near,
        gain,
        hidden,
        grads,
        grads_near,
    )
    grad_head = lax.dot_general(
        logit_grads, hidden, (((1,), (0,)), ((), ())), preferred_element_type=f32
    ).astype(bf16)
    plane = kernel_call(
        part(column_kernel, nvoc),
        [((nmod, cols + size), bf16)] * nchip,
        attn_values,
        *column,
    )
    plane = swaps(plane, "rows", 2)
    (main,) = kernel_call(main_kernel, [((tok, width), bf16)], *main)
    near = swap(main, "vocab", 1)
    module, own_values = kernel_call(
        part(plane_kernel, tok, nchip),
        [((nmod, cols + hdim), bf16), ((nmod, hdim), bf16)],
        *plane,
    )
    (main,) = kernel_call(main_kernel, [((tok, width), bf16)], main, near)
    main = [main, swap(main, "vocab", 2)]
    other = swap(module, "rows", 1)
    residual, values, *parcels = kernel_call(
        part(last_kernel, tok),
        [((ntok, cols), bf16), ((ntok, hdim), bf16)]
        + [((tok_voc, cols * tok // tok_voc + 3 * hdim), bf16)] * nvoc,
        raw,
        raw_near,
        inverse,
        dot_mean,
        gain,
        out_proj,
        module,
        other,
        own_values,
        side=[pltpu.VMEM((ntok, hdim), f32)],
    )
    parcels = swaps(parcels, "vocab", 1)
    (grad_out_proj,) = kernel_call(proj_kernel, [((hdim, cols), bf16)], values, residual)
    grad_trunk, grad_residual, grad_gain, grad_attn = kernel_call(
        part(output_kernel, tok, nvoc, cols),
        [
            ((tok, width), bf16),
            ((tok, width), bf16),
            ((1, width), f32),
            ((tok_voc, hdim // size, size), bf16),
        ],
        grad_head,
        *parcels,
        *main,
        away=(0,),
    )
    return (
        grad_trunk,
        grad_residual,
        grad_gain.reshape(width),
        grad_head,
        grad_attn,
        grad_out_proj,
    )


def swaps(parts, axis, unit):
    got = [parts[0]]
    for k in range(1, len(parts)):
        got.append(swap(parts[k], axis, k * unit))
    return got


def choose(*args):
    tok, cols, hdim = args[0].shape[0], args[7].shape[1], args[7].shape[0]
    ntok = lax.axis_size("rows") * tok
    tok_voc = ntok // lax.axis_size("vocab")
    fits = (
        lax.axis_size("rows") == 8
        and ntok == 32
        and         tok_voc == 8
        and lax.axis_size("vocab") == 4
        and tok_voc % tok == 0
        and cols % (128 * tok_voc // tok) == 0
        and hdim % 128 == 0
        and cols % hdim == 0
        and cols // hdim <= tok_voc
        and args[6].shape[1] // (lax.axis_size("rows") // 2) == tok
    )
    if not fits:
        return plain(*args)
    return local(*args)


def solution(mesh):
    return jax.shard_map(
        choose,
        mesh=mesh,
        in_specs=(
            P("rows", None),
            P("rows", None),
            P(),
            P(("vocab", "rows"), None),
            P(),
            P(),
            P("rows", None, None),
            P("rows", "vocab"),
        ),
        out_specs=(
            P("rows", None),
            P("rows", None),
            P(),
            P(("vocab", "rows"), None),
            P("vocab", "rows", None),
            P("rows", "vocab"),
        ),
        check_vma=False,
    )
```
